32 devices in a mesh: cols: 8 (over z, x), rows: 4 (over y, core).
Axes of the slice: x: 2, y: 2, z: 4, core: 2. Of those that a mesh axis runs over, the one named last changes fastest.
Arguments:
- slide_pixels: bfloat16 [3, 1024, 4096], P(None, 'rows', 'cols'), may hold values from -6 to 6
- stem_first: bfloat16 [6, 6, 3, 64], replicated, may hold values from -0.625 to 0.625
- stem_second: bfloat16 [6, 6, 64, 256], replicated, may hold values from -0.125 to 0.125
- stem_third: bfloat16 [3, 3, 256, 1024], replicated, may hold values from -0.125 to 0.125
- key_weight: bfloat16 [1024, 1024], replicated, may hold values from -0.1875 to 0.1875
- value_weight: bfloat16 [1024, 1024], replicated, may hold values from -0.1875 to 0.1875
- queries: bfloat16 [512, 1024], replicated, may hold values from -240 to 240
Outputs:
- attended: bfloat16 [512, 1024], P(('cols', 'rows'))
The draws below stay inside these ranges and needn't reach their ends.
All inputs are finite; a program needn't handle non-finite values.
Results may differ from the reference program's by a relative error of at most 0.033.
Values may be sent and summed in bfloat16 or wider, within the bound.
No kernel may reach another device: no remote copies, remote signals or barrier semaphores. Data moves between devices by JAX's collectives and lax.ppermute only.
A program may use at most 128 MiB of HBM per device.

```python
import math
import jax
import jax.numpy as jnp
from jax import lax

D = 1024
HEADS = 8
LATENTS = 512
C1 = 64
C2 = 256
TILE_ROWS = 8
TILE_COLS = 16
DH = 128
IH = 1024
IW = 4096
N_ROWS = 4


def draw_queries(key, part):
    base_draw = jnp.clip(jax.random.normal(jax.random.fold_in(key, 11), (LATENTS, D), jnp.float32), -4.0, 4.0)
    return (4.0 * base_draw).astype(jnp.bfloat16)


def level_of(rng, extent, pieces, low, top_value):
    factor_of = 1.0
    for dim, shards_of in pieces:
        steps = jax.random.uniform(jax.random.fold_in(jax.random.fold_in(rng, 6), dim), (shards_of,), jnp.float32, low / len(pieces), top_value / len(pieces))
        factor_of = factor_of * jnp.repeat(jnp.exp(steps), extent[dim] // shards_of).reshape((-1,) + (1,) * (len(extent) - 1 - dim))
    return factor_of


def bell_draw(own_key, shape, scale, bound, cuts=(), kind=jnp.bfloat16):
    values = scale * jax.random.normal(own_key, shape, jnp.float32)
    if cuts:
        values = values * level_of(own_key, shape, cuts, -0.22, 0.18)
    return jnp.clip(values, -bound, bound).astype(kind)


def setup_inputs(seed: int = 0) -> dict:
    streams_of = jax.random.split(jax.random.key(seed), 8)
    slide_pixels = bell_draw(streams_of[0], (3, IH, IW), 1.0, 6.0, ((1, 4), (2, 8)))
    stem_first = bell_draw(streams_of[1], (6, 6, 3, C1), 108 ** -0.5, 0.625)
    stem_second = bell_draw(streams_of[2], (6, 6, C1, C2), (36 * C1) ** -0.5, 0.125)
    stem_third = bell_draw(streams_of[3], (3, 3, C2, D), (9 * C2) ** -0.5, 0.125)
    key_weight = bell_draw(streams_of[4], (D, D), D ** -0.5, 0.1875)
    value_weight = bell_draw(streams_of[5], (D, D), D ** -0.5, 0.1875)
    queries = draw_queries(jax.random.fold_in(streams_of[7], 71), 0)
    return dict(slide_pixels=slide_pixels, stem_first=stem_first, stem_second=stem_second, stem_third=stem_third, key_weight=key_weight, value_weight=value_weight, queries=queries)


def stem_map(slide_pixels, stem_first, stem_second, stem_third):
    first_map = lax.conv_general_dilated(slide_pixels[None], stem_first, (4, 4), ((1, 1), (1, 1)), dimension_numbers=('NCHW', 'HWIO', 'NCHW'), preferred_element_type=jnp.float32)
    first_map = jax.nn.gelu(first_map).astype(jnp.bfloat16)
    second_map = lax.conv_general_dilated(first_map, stem_second, (4, 4), ((1, 1), (1, 1)), dimension_numbers=('NCHW', 'HWIO', 'NHWC'), preferred_element_type=jnp.float32)
    second_map = jax.nn.gelu(second_map).astype(jnp.bfloat16)
    third_map = lax.conv_general_dilated(second_map, stem_third, (2, 2), ((1, 1), (1, 1)), dimension_numbers=('NHWC', 'HWIO', 'NHWC'), preferred_element_type=jnp.float32)
    return third_map[0]

def norm_rows(features):
    tok_mean = lax.optimization_barrier(jnp.mean(features, axis=-1, keepdims=True))
    centred = features - tok_mean
    tok_var = lax.optimization_barrier(jnp.mean(centred * centred, axis=-1, keepdims=True))
    return (centred * lax.rsqrt(tok_var + 1e-05)).astype(jnp.bfloat16)

def reference(slide_pixels, stem_first, stem_second, stem_third, key_weight, value_weight, queries):
    third_map = stem_map(slide_pixels, stem_first, stem_second, stem_third)
    normed = norm_rows(third_map.reshape(-1, D))
    key_rows = lax.optimization_barrier(jnp.dot(normed, key_weight, preferred_element_type=jnp.float32).astype(jnp.bfloat16))
    value_rows = lax.optimization_barrier(jnp.dot(normed, value_weight, preferred_element_type=jnp.float32).astype(jnp.bfloat16))
    block_len = TILE_ROWS * TILE_COLS * N_ROWS
    key_blocks = key_rows.reshape(-1, block_len, HEADS, DH)
    value_blocks = value_rows.reshape(-1, block_len, HEADS, DH)
    query_heads = queries.reshape(LATENTS, HEADS, DH).astype(jnp.float32)
    score_scale = 1.0 / math.sqrt(DH)

    def block_scores(key_block):
        return jnp.einsum('lhd,thd->hlt', query_heads, key_block.astype(jnp.float32)) * score_scale

    def block_peak(key_block):
        return lax.optimization_barrier(jnp.max(block_scores(key_block), axis=2))
    peak_score = lax.optimization_barrier(jnp.max(lax.map(block_peak, key_blocks), axis=0))

    def accumulate(running, blocks):
        row_total, weighted = running
        weights = jnp.exp(block_scores(blocks[0]) - peak_score[:, :, None])
        rounded = lax.optimization_barrier(weights.astype(jnp.bfloat16))
        weighted = weighted + jnp.einsum('hlt,thd->lhd', rounded.astype(jnp.float32), blocks[1].astype(jnp.float32))
        return ((row_total + lax.optimization_barrier(jnp.sum(weights, axis=2)), weighted), None)
    start_state = (jnp.zeros((HEADS, LATENTS), jnp.float32), jnp.zeros((LATENTS, HEADS, DH), jnp.float32))
    final_state, unused = lax.scan(accumulate, start_state, (key_blocks, value_blocks))
    row_total, weighted = final_state
    attended = weighted / row_total.T[:, :, None]
    return attended.reshape(LATENTS, D).astype(jnp.bfloat16)
```

```python
import functools
import math

import jax
import jax.numpy as jnp
from jax import lax
from jax.experimental import pallas as pl
from jax.experimental.pallas import tpu as pltpu
from jax.sharding import PartitionSpec as P

HEADS = 8
BEFORE, AFTER = 21, 5
TAPS1 = 18
BLOCK_COLS = 28
BLOCKS = 5
BLOCK_LANES = BLOCK_COLS * 64
ROWS1 = 80
ROWS2 = 24
COLS2 = 34
STAT = 128
VMEM = pltpu.MemorySpace.VMEM


def gelu(x):
    inner = x * (0.7978845608028654 + 0.035677408136300125 * (x * x))
    half = 0.5 * x
    return half + half * jnp.tanh(inner)


def lanes_of(shape):
    return lax.broadcasted_iota(jnp.int32, shape, len(shape) - 1)


def col_edges_kernel(lo_ref, hi_ref, a_ref, b_ref):
    even = lax.axis_index("cols") % 2 == 0
    lane = lanes_of((128, 128))
    first = jnp.zeros((128, 128), jnp.float32)
    last = jnp.zeros((128, 128), jnp.float32)
    for c in range(3):
        for half in range(2):
            g = BEFORE * (2 * c + half)
            rows = slice(half * 128, half * 128 + 128)
            lo = lo_ref[c, rows, :].astype(jnp.float32)
            hi = hi_ref[c, rows, :].astype(jnp.float32)
            lo = pltpu.roll(lo, g, 1) if g else lo
            hi = pltpu.roll(hi, (g + BEFORE) % 128, 1)
            first = jnp.where((lane >= g) & (lane < g + AFTER), lo, first)
            last = jnp.where((lane >= g) & (lane < g + BEFORE), hi, last)
    a_ref[...] = jnp.where(even, last, first).astype(jnp.bfloat16)
    b_ref[...] = jnp.where(even, first, last).astype(jnp.bfloat16)


def row_edges_kernel(top_ref, bottom_ref, ca_ref, cb_ref, a_ref, b_ref):
    even_col = lax.axis_index("cols") % 2 == 0
    even = lax.axis_index("rows") % 2 == 0
    ca = ca_ref[...].astype(jnp.float32)
    cb = cb_ref[...].astype(jnp.float32)
    left = jnp.where(even_col, cb, ca)
    right = jnp.where(even_col, ca, cb)
    lane = lanes_of((24, 128))
    for c in range(3):
        pieces = []
        for half, rows, main in ((0, slice(0, 24), top_ref[c, 0:24, :]), (1, slice(104, 128), bottom_ref[c, 8:32, :])):
            g = BEFORE * (2 * c + half)
            lt = pltpu.roll(left[rows], (128 - g) % 128, 1) if g else left[rows]
            rt = pltpu.roll(right[rows], (128 - g + BEFORE) % 128, 1)
            side = jnp.where(lane < BEFORE, lt, jnp.where(lane < BEFORE + AFTER, rt, 0.0))
            pieces.append((main.astype(jnp.float32), side))
        (top_main, top_side), (bottom_main, bottom_side) = pieces
        a_ref[c, :, 0:512] = jnp.where(even, bottom_main, top_main).astype(jnp.bfloat16)
        b_ref[c, :, 0:512] = jnp.where(even, top_main, bottom_main).astype(jnp.bfloat16)
        a_ref[c, :, 512:640] = jnp.where(even, bottom_side, top_side).astype(jnp.bfloat16)
        b_ref[c, :, 512:640] = jnp.where(even, top_side, bottom_side).astype(jnp.bfloat16)


def windows(xb_ref, c, row0, main, left, right):
    n = main.shape[0]
    lane = lanes_of((n, 128))
    moved = pltpu.roll(main, BEFORE, 1)
    tiles = [moved[:, 128 * k : 128 * k + 128] for k in range(4)]
    tail = jnp.where(lane < BEFORE, tiles[0], jnp.where(lane < BEFORE + AFTER, right, 0.0))
    tiles = [jnp.where(lane < BEFORE, left, tiles[0])] + tiles[1:] + [tail]
    xb_ref[0, c, pl.ds(row0, n), :] = tiles[0]
    for b in range(1, BLOCKS):
        t, s = divmod(4 * BLOCK_COLS * b, 128)
        early = pltpu.roll(tiles[t], 128 - s, 1)
        late = pltpu.roll(tiles[t + 1], 128 - s, 1)
        xb_ref[b, c, pl.ds(row0, n), :] = jnp.where(lane < 128 - s, early, late)


def main_kernel(
    ca_ref, cb_ref, ra_ref, rb_ref, taps_ref, slide_hbm, w2_hbm, w3_hbm, wk_hbm, wv_hbm, q_hbm,
    keep_ref, send_ref,
    slide, w2, w3, wk, wv, q, sems, toep, xb, lhs1, fmap, lhs2, smap, lhs3, third, kbd, vbd, out,
    *, col_last, row_last,
):
    col = lax.axis_index("cols")
    row = lax.axis_index("rows")
    copies = [
        pltpu.make_async_copy(src, dst, sems.at[i])
        for i, (src, dst) in enumerate(
            ((slide_hbm, slide), (w2_hbm, w2), (w3_hbm, w3), (wk_hbm, wk), (wv_hbm, wv), (q_hbm, q))
        )
    ]
    for copy in copies:
        copy.start()

    def band(k, carry):
        base = pl.multiple_of(k * 128, 128)
        toep[pl.ds(base, 128), :] = jnp.zeros((128, BLOCK_LANES), jnp.bfloat16)
        p0 = taps_ref[k, 0:16, :]
        p1 = taps_ref[k, 16:32, :]
        p2 = taps_ref[k, 32:48, :]
        for m in range(BLOCK_LANES // 256):
            toep[pl.ds(base + 16 * m, 16), 256 * m : 256 * m + 128] = p0
            toep[pl.ds(base + 16 * m, 16), 256 * m + 128 : 256 * m + 256] = p1
            toep[pl.ds(base + 16 * m + 16, 16), 256 * m + 128 : 256 * m + 256] = p2
        return carry

    lax.fori_loop(0, TAPS1, band, 0)

    even_col = col % 2 == 0
    even_row = row % 2 == 0
    copies[0].wait()
    for c in range(3):
        above = jnp.where(even_row, rb_ref[c].astype(jnp.float32), ra_ref[c].astype(jnp.float32))
        below = jnp.where(even_row, ra_ref[c].astype(jnp.float32), rb_ref[c].astype(jnp.float32))[0:8]
        windows(xb, c, 0, above[:, 0:512], above[:, 512:640], above[:, 512:640])
        windows(xb, c, 280, below[:, 0:512], below[:, 512:640], below[:, 512:640])
        for b in range(BLOCKS):
            xb[b, c, 288:328, :] = jnp.zeros((40, 128), jnp.float32)
        for half in range(2):
            g = BEFORE * (2 * c + half)

            def part(k, carry, c=c, half=half, g=g):
                r = pl.multiple_of(k * 32, 32)
                ca = ca_ref[pl.ds(r, 32), :].astype(jnp.float32)
                cb = cb_ref[pl.ds(r, 32), :].astype(jnp.float32)
                left = jnp.where(even_col, cb, ca)
                right = jnp.where(even_col, ca, cb)
                left = pltpu.roll(left, 128 - g, 1) if g else left
                right = pltpu.roll(right, (128 - g + BEFORE) % 128, 1)
                main = slide[c, pl.ds(half * 128 + r, 32), :].astype(jnp.float32)
                windows(xb, c, half * 128 + 24 + r, main, left, right)
                return carry

            lax.fori_loop(0, 4, part, 0)

    for b in range(BLOCKS):
        for c in range(3):
            for kh in range(6):
                k = 6 * c + kh
                lhs1[ROWS1 * b : ROWS1 * b + ROWS1, 128 * k : 128 * k + 128] = xb[
                    b, c, pl.ds(24 - BEFORE + kh, ROWS1, stride=4), :
                ].astype(jnp.bfloat16)

    def first(n, carry):
        lanes = pl.ds(pl.multiple_of(n * 256, 256), 256)
        acc = gelu(jnp.dot(lhs1[...], toep[:, lanes], preferred_element_type=jnp.float32))
        for b in range(BLOCKS):
            for u in range(2):
                fmap[b, 2 * n + u, 0:ROWS1, :] = acc[ROWS1 * b : ROWS1 * b + ROWS1, 128 * u : 128 * u + 128]
        return carry

    lax.fori_loop(0, BLOCK_LANES // 256, first, 0)

    @pl.when(row == 0)
    def _():
        for b in range(BLOCKS):
            fmap[b, :, 0:5, :] = jnp.zeros((BLOCK_LANES // 128, 5, 128), jnp.float32)

    @pl.when(row == row_last)
    def _():
        for b in range(BLOCKS):
            fmap[b, :, 69:70, :] = jnp.zeros((BLOCK_LANES // 128, 1, 128), jnp.float32)

    @pl.when(col == 0)
    def _():
        fmap[0, 0:2, 0:ROWS1, :] = jnp.zeros((2, ROWS1, 128), jnp.float32)
        fmap[0, 2, 0:ROWS1, 0:64] = jnp.zeros((ROWS1, 64), jnp.float32)

    @pl.when(col == col_last)
    def _():
        tile, side = divmod(133 - 4 * BLOCK_COLS, 2)
        fmap[4, tile, 0:ROWS1, 64 * side : 64 * side + 64] = jnp.zeros((ROWS1, 64), jnp.float32)

    for kh in range(6):
        for pair in range(COLS2 // 2):
            both = []
            for j in (2 * pair, 2 * pair + 1):
                b, t = divmod(j, 7)
                rows = pl.ds(kh, ROWS2, stride=4)
                tiles = [divmod(14 * b + 2 * t + u, 14) for u in range(3)]
                both.append([fmap[block, tile, rows, :] for block, tile in tiles])
            for u in range(3):
                lhs2[48 * pair : 48 * pair + 48, 384 * kh + 128 * u : 384 * kh + 128 * u + 128] = jnp.concatenate(
                    [both[0][u], both[1][u]], axis=0
                ).astype(jnp.bfloat16)
    copies[1].wait()
    for start, size in ((0, 288), (288, 288), (576, 240)):
        acc = gelu(jnp.dot(lhs2[start : start + size, :], w2[...], preferred_element_type=jnp.float32))
        for u in range(2):
            smap[u, start // ROWS2 : (start + size) // ROWS2] = acc[:, 128 * u : 128 * u + 128].reshape(
                size // ROWS2, ROWS2, 128
            )

    @pl.when(row == 0)
    def _():
        smap[:, :, 0:1, :] = jnp.zeros((2, COLS2, 1, 128), jnp.float32)

    @pl.when(col == 0)
    def _():
        smap[:, 0] = jnp.zeros((2, ROWS2, 128), jnp.float32)

    for kh in range(3):
        for kw in range(3):
            k = 3 * kh + kw
            for pair in range(8):
                for u in range(2):
                    lhs3[16 * pair : 16 * pair + 16, 256 * k + 128 * u : 256 * k + 128 * u + 128] = jnp.concatenate(
                        [
                            smap[u, 4 * pair + 2 * v + kw, pl.ds(kh, 8, stride=2), :]
                            for v in range(2)
                        ],
                        axis=0,
                    ).astype(jnp.bfloat16)
    copies[2].wait()

    def conv3(n, carry):
        lanes = pl.ds(pl.multiple_of(n * 256, 256), 256)
        third[:, lanes] = jnp.dot(lhs3[...], w3[:, lanes], preferred_element_type=jnp.float32)
        return carry

    lax.fori_loop(0, 4, conv3, 0)
    tokens = third[...]
    centred = tokens - jnp.mean(tokens, axis=-1, keepdims=True)
    var = jnp.mean(centred * centred, axis=-1, keepdims=True)
    normed = (centred * lax.rsqrt(var + 1e-05)).astype(jnp.bfloat16)
    lhs3[:, 0:1024] = normed
    copies[3].wait()
    copies[4].wait()
    low = lanes_of((128, 256)) < 128

    def project(n, carry):
        lanes = pl.ds(pl.multiple_of(n * 256, 256), 256)
        for w, dst in ((wk, kbd), (wv, vbd)):
            rows = jnp.dot(lhs3[:, 0:1024], w[:, lanes], preferred_element_type=jnp.float32)
            dst[n, 0:128, :] = jnp.where(low, rows, 0.0).astype(jnp.bfloat16)
            dst[n, 128:256, :] = jnp.where(low, 0.0, rows).astype(jnp.bfloat16)
        return carry

    lax.fori_loop(0, 4, project, 0)
    copies[5].wait()
    scale = 1.0 / math.sqrt(128)
    latents = out.shape[0]
    step = 128

    def attend(i, carry):
        rows = pl.ds(pl.multiple_of(i * step, step), step)
        lane = lanes_of((step, 128))
        stat = jnp.zeros((step, 128), jnp.float32)
        for n in range(4):
            scores = lax.dot_general(
                q[rows, 256 * n : 256 * n + 256], kbd[n], (((1,), (1,)), ((), ())), preferred_element_type=jnp.float32
            ) * scale
            probs, recips = [], []
            for u in range(2):
                s = scores[:, 128 * u : 128 * u + 128]
                peak = jnp.max(s, axis=1, keepdims=True)
                w = jnp.exp(s - peak)
                total = jnp.sum(w, axis=1, keepdims=True)
                probs.append(w.astype(jnp.bfloat16))
                recips.append(1.0 / total)
                stat = jnp.where(lane == 2 * n + u, peak + jnp.log(total), stat)
            o = jnp.dot(jnp.concatenate(probs, axis=1), vbd[n], preferred_element_type=jnp.float32)
            out[rows, 256 * n : 256 * n + 128] = o[:, 0:128] * recips[0]
            out[rows, 256 * n + 128 : 256 * n + 256] = o[:, 128:256] * recips[1]
        out[rows, 1024:1152] = stat
        return carry

    lax.fori_loop(0, latents // step, attend, 0)
    half = latents // 2
    bit = row % 2
    keep_ref[...] = out[pl.ds(pl.multiple_of(bit * half, half), half), :]
    other = pl.ds(pl.multiple_of((1 - bit) * half, half), half)
    send_ref[:, 0:1024] = out[other, 0:1024].astype(jnp.bfloat16)
    send_ref[:, 1024:1152] = pack_stat(out[other, 1024:1152])


def pack_stat(stat):
    lane = lanes_of(stat.shape)
    stat = jnp.where(lane < HEADS, stat, 0.0)
    high = stat.astype(jnp.bfloat16).astype(jnp.float32)
    rest = stat - high
    mid = rest.astype(jnp.bfloat16).astype(jnp.float32)
    low = rest - mid
    return (high + pltpu.roll(mid, HEADS, 1) + pltpu.roll(low, 2 * HEADS, 1)).astype(jnp.bfloat16)


def unpack_stat(stat):
    stat = stat.astype(jnp.float32)
    return stat + pltpu.roll(stat, 128 - HEADS, 1) + pltpu.roll(stat, 128 - 2 * HEADS, 1)


def merge_kernel(keep_ref, recv_ref, *outs, bit_of):
    n = keep_ref.shape[0]
    mine = keep_ref[:, 1024:1152]
    theirs = unpack_stat(recv_ref[:, 1024:1152])
    peak = jnp.maximum(mine, theirs)
    em = jnp.exp(mine - peak)
    total = em + jnp.exp(theirs - peak)
    share = em / total
    stat = peak + jnp.log(total)
    merged = []
    for h in range(HEADS):
        lanes = slice(128 * h, 128 * h + 128)
        a = keep_ref[:, lanes]
        b = recv_ref[:, lanes].astype(jnp.float32)
        merged.append(b + jnp.broadcast_to(share[:, h : h + 1], (n, 128)) * (a - b))
    if bit_of is None:
        for h in range(HEADS):
            outs[0][:, 128 * h : 128 * h + 128] = merged[h].astype(jnp.bfloat16)
        return
    upper = bit_of() == 1
    half = n // 2
    for h in range(HEADS):
        lanes = slice(128 * h, 128 * h + 128)
        outs[0][:, lanes] = jnp.where(upper, merged[h][half:], merged[h][:half])
        outs[1][:, lanes] = jnp.where(upper, merged[h][:half], merged[h][half:]).astype(jnp.bfloat16)
    outs[0][:, 1024:1152] = jnp.where(upper, stat[half:], stat[:half])
    outs[1][:, 1024:1152] = pack_stat(jnp.where(upper, stat[:half], stat[half:]))


def merge(keep, recv, bit_of):
    n, width = keep.shape
    if bit_of is None:
        shapes = jax.ShapeDtypeStruct((n, 1024), jnp.bfloat16)
    else:
        shapes = (
            jax.ShapeDtypeStruct((n // 2, width), jnp.float32),
            jax.ShapeDtypeStruct((n // 2, width), jnp.bfloat16),
        )
    return pl.pallas_call(functools.partial(merge_kernel, bit_of=bit_of), out_shape=shapes, name="merge")(keep, recv)


def swap_pairs(size, odd):
    pairs = []
    for i in range(1 if odd else 0, size - 1, 2):
        pairs += [(i, i + 1), (i + 1, i)]
    return pairs


def bits_of(size):
    return size.bit_length() - 1


def plan(mesh):
    n_rows, n_cols = mesh.shape["rows"], mesh.shape["cols"]
    row_bits = [("rows", k) for k in range(1, bits_of(n_rows))]
    col_bits = [("cols", k) for k in range(bits_of(n_cols))]
    return row_bits + col_bits, col_bits[:1] + row_bits + col_bits[1:]


def solution(mesh):
    n_rows, n_cols = mesh.shape["rows"], mesh.shape["cols"]
    orders = plan(mesh)

    def partner(index, stage):
        col, row = divmod(index, n_rows)
        if stage < 0:
            return col * n_rows + (row ^ 1)
        axis, k = orders[row & 1][stage]
        return col * n_rows + (row ^ (1 << k)) if axis == "rows" else (col ^ (1 << k)) * n_rows + row

    def exchange(value, stage):
        pairs = [(i, partner(i, stage)) for i in range(n_rows * n_cols)]
        return lax.ppermute(value, ("cols", "rows"), pairs)

    def bit_of(stage):
        def read():
            row = lax.axis_index("rows")
            (axis0, k0), (axis1, k1) = orders[0][stage], orders[1][stage]
            return jnp.where(
                row % 2 == 0, (lax.axis_index(axis0) >> k0) & 1, (lax.axis_index(axis1) >> k1) & 1
            )

        return read

    def order_queries(queries):
        latents, width = queries.shape
        share = latents // (n_rows * n_cols)
        names = [("cols", k) for k in reversed(range(bits_of(n_cols)))]
        names += [("rows", k) for k in reversed(range(bits_of(n_rows)))]
        split = queries.reshape([2] * len(names) + [share, width])
        at = names.index(("rows", 0))
        rest = names[:at] + names[at + 1 :]
        halves = []
        for core in range(2):
            part = lax.index_in_dim(split, core, at, keepdims=False)
            axes = [rest.index(name) for name in orders[core]]
            halves.append(part.transpose(axes + [len(rest), len(rest) + 1]).reshape(latents // 2, width))
        return jnp.concatenate(halves, axis=0)

    def on_device(slide_pixels, stem_first, stem_second, stem_third, key_weight, value_weight, queries):
        bf16 = jnp.bfloat16
        edge = jax.ShapeDtypeStruct((128, 128), bf16)
        col_a, col_b = pl.pallas_call(
            col_edges_kernel,
            grid=(1,),
            in_specs=[
                pl.BlockSpec((3, 256, 128), lambda i: (0, 0, 0)),
                pl.BlockSpec((3, 256, 128), lambda i: (0, 0, 3)),
            ],
            out_specs=[pl.BlockSpec((128, 128), lambda i: (0, 0))] * 2,
            out_shape=(edge, edge),
            name="col_edges",
        )(slide_pixels, slide_pixels)
        col_a = lax.ppermute(col_a, "cols", swap_pairs(n_cols, False))
        col_b = lax.ppermute(col_b, "cols", swap_pairs(n_cols, True))
        rim = jax.ShapeDtypeStruct((3, 24, 640), bf16)
        row_a, row_b = pl.pallas_call(
            row_edges_kernel,
            grid=(1,),
            in_specs=[
                pl.BlockSpec((3, 32, 512), lambda i: (0, 0, 0)),
                pl.BlockSpec((3, 32, 512), lambda i: (0, 7, 0)),
                pl.BlockSpec((128, 128), lambda i: (0, 0)),
                pl.BlockSpec((128, 128), lambda i: (0, 0)),
            ],
            out_specs=[pl.BlockSpec((3, 24, 640), lambda i: (0, 0, 0))] * 2,
            out_shape=(rim, rim),
            name="row_edges",
        )(slide_pixels, slide_pixels, col_a, col_b)
        row_a = lax.ppermute(row_a, "rows", swap_pairs(n_rows, False))
        row_b = lax.ppermute(row_b, "rows", swap_pairs(n_rows, True))

        taps = stem_first.transpose(2, 0, 1, 3).reshape(TAPS1, 6, 64)
        taps = sum(
            jnp.pad(taps, ((0, 0), (top, 42 - top), (64 * side, 64 - 64 * side)))
            for top, side in ((0, 0), (4, 1), (24, 0), (28, 1))
        )
        latents = queries.shape[0]
        half = latents // 2
        any_spec = pl.BlockSpec(memory_space=pl.ANY)
        vmem_spec = pl.BlockSpec(memory_space=VMEM)
        keep, send = pl.pallas_call(
            functools.partial(main_kernel, col_last=n_cols - 1, row_last=n_rows - 1),
            in_specs=[vmem_spec] * 5 + [any_spec] * 6,
            out_specs=[vmem_spec] * 2,
            out_shape=(
                jax.ShapeDtypeStruct((half, 1024 + STAT), jnp.float32),
                jax.ShapeDtypeStruct((half, 1024 + STAT), bf16),
            ),
            scratch_shapes=[
                pltpu.VMEM((3, 256, 512), bf16),
                pltpu.VMEM((2304, 256), bf16),
                pltpu.VMEM((2304, 1024), bf16),
                pltpu.VMEM((1024, 1024), bf16),
                pltpu.VMEM((1024, 1024), bf16),
                pltpu.VMEM((latents, 1024), bf16),
                pltpu.SemaphoreType.DMA((6,)),
                pltpu.VMEM((TAPS1 * 128, BLOCK_LANES), bf16),
                pltpu.VMEM((BLOCKS, 3, 328, 128), jnp.float32),
                pltpu.VMEM((BLOCKS * ROWS1, TAPS1 * 128), bf16),
                pltpu.VMEM((BLOCKS, BLOCK_LANES // 128, 104, 128), jnp.float32),
                pltpu.VMEM((COLS2 * ROWS2, 2304), bf16),
                pltpu.VMEM((2, COLS2, ROWS2, 128), jnp.float32),
                pltpu.VMEM((128, 2304), bf16),
                pltpu.VMEM((128, 1024), jnp.float32),
                pltpu.VMEM((4, 256, 256), bf16),
                pltpu.VMEM((4, 256, 256), bf16),
                pltpu.VMEM((latents, 1024 + STAT), jnp.float32),
            ],
            compiler_params=pltpu.CompilerParams(vmem_limit_bytes=60 * 1024 * 1024),
            name="read",
        )(
            col_a, col_b, row_a, row_b, taps, slide_pixels,
            stem_second.reshape(2304, 256), stem_third.reshape(2304, 1024),
            key_weight, value_weight, order_queries(queries),
        )
        recv = exchange(send, -1)
        stages = len(orders[0])
        for stage in range(stages):
            keep, send = merge(keep, recv, bit_of(stage))
            recv = exchange(send, stage)
        return merge(keep, recv, None)

    placed = (P(None, "rows", "cols"), P(), P(), P(), P(), P(), P())
    return jax.shard_map(
        on_device, mesh=mesh, in_specs=placed, out_specs=P(("cols", "rows"), None), check_vma=False
    )
```

```python
import functools
import math

import jax
import jax.numpy as jnp
from jax import lax
from jax.experimental import pallas as pl
from jax.experimental.pallas import tpu as pltpu
from jax.sharding import PartitionSpec as P

HEADS = 8
BEFORE, AFTER = 21, 5
TAPS1 = 18
BLOCK_COLS = 28
BLOCKS = 5
BLOCK_LANES = BLOCK_COLS * 64
ROWS1 = 80
ROWS2 = 24
COLS2 = 34
STAT = 128
RIM = 24
STRIP = 144
VMEM = pltpu.MemorySpace.VMEM


def gelu(x):
    inner = x * (0.7978845608028654 + 0.035677408136300125 * (x * x))
    half = 0.5 * x
    return half + half * jnp.tanh(inner)


def lanes_of(shape):
    return lax.broadcasted_iota(jnp.int32, shape, len(shape) - 1)


def row_edges_kernel(slide, a_ref, b_ref):
    even = lax.axis_index("rows") % 2 == 0
    for c in range(3):
        top = slide[c, 0:RIM, :]
        bottom = slide[c, 224:256, :].astype(jnp.float32)[8:32].astype(jnp.bfloat16)

        @pl.when(even)
        def _():
            a_ref[c] = bottom
            b_ref[c] = top

        @pl.when(jnp.logical_not(even))
        def _():
            a_ref[c] = top
            b_ref[c] = bottom


def rims(c, ra_ref, rb_ref, lanes):
    even = lax.axis_index("rows") % 2 == 0
    ra = ra_ref[c, :, lanes].astype(jnp.float32)
    rb = rb_ref[c, :, lanes].astype(jnp.float32)
    return jnp.where(even, rb, ra), jnp.where(even, ra, rb)[0:8]


def col_edges_kernel(slide, ra_ref, rb_ref, a_ref, b_ref):
    even = lax.axis_index("cols") % 2 == 0
    lane = lanes_of((STRIP, 128))
    first = jnp.zeros((STRIP, 128), jnp.float32)
    last = jnp.zeros((STRIP, 128), jnp.float32)
    for c in range(3):
        sides = []
        for lanes in (slice(0, 128), slice(384, 512)):
            above, below = rims(c, ra_ref, rb_ref, lanes)
            sides.append(jnp.concatenate([above, slide[c, :, lanes].astype(jnp.float32), below], axis=0))
        for half in range(2):
            g = BEFORE * (2 * c + half)
            rows = slice(half * STRIP, half * STRIP + STRIP)
            lo = pltpu.roll(sides[0][rows], g, 1) if g else sides[0][rows]
            hi = pltpu.roll(sides[1][rows], (g + BEFORE) % 128, 1)
            first = jnp.where((lane >= g) & (lane < g + AFTER), lo, first)
            last = jnp.where((lane >= g) & (lane < g + BEFORE), hi, last)
    a_ref[...] = jnp.where(even, last, first).astype(jnp.bfloat16)
    b_ref[...] = jnp.where(even, first, last).astype(jnp.bfloat16)


def band_kernel(taps_ref, toep):
    def band(k, carry):
        base = pl.multiple_of(k * 128, 128)
        toep[pl.ds(base, 128), :] = jnp.zeros((128, BLOCK_LANES), jnp.bfloat16)
        p0 = taps_ref[k, 0:16, :]
        p1 = taps_ref[k, 16:32, :]
        p2 = taps_ref[k, 32:48, :]
        for m in range(BLOCK_LANES // 256):
            toep[pl.ds(base + 16 * m, 16), 256 * m : 256 * m + 128] = p0
            toep[pl.ds(base + 16 * m, 16), 256 * m + 128 : 256 * m + 256] = p1
            toep[pl.ds(base + 16 * m + 16, 16), 256 * m + 128 : 256 * m + 256] = p2
        return carry

    lax.fori_loop(0, TAPS1, band, 0)


def windows(refs, c, row0, main):
    n = main.shape[0]
    lane = lanes_of((n, 128))
    moved = pltpu.roll(main, BEFORE, 1)
    tiles = [moved[:, 128 * k : 128 * k + 128] for k in range(4)]
    tiles.append(jnp.where(lane < BEFORE, tiles[0], 0.0))
    for b, (ref, at) in enumerate(refs):
        t, s = divmod(4 * BLOCK_COLS * b, 128)
        value = tiles[t]
        if s:
            value = jnp.where(lane < 128 - s, pltpu.roll(value, 128 - s, 1), pltpu.roll(tiles[t + 1], 128 - s, 1))
        ref[at, c, pl.ds(row0, n), :] = value


def patch_rows(ref, at, lhs1, slot):
    for c in range(3):
        for kh in range(6):
            k = 6 * c + kh
            lhs1[ROWS1 * slot : ROWS1 * slot + ROWS1, 128 * k : 128 * k + 128] = ref[
                at, c, pl.ds(RIM - BEFORE + kh, ROWS1, stride=4), :
            ].astype(jnp.bfloat16)


def inner_kernel(slide, ra_ref, rb_ref, toep, edge, fmap, inner, lhs1):
    refs = [(edge, 0), (inner, 0), (inner, 1), (inner, 2), (edge, 1)]
    for c in range(3):
        above, below = rims(c, ra_ref, rb_ref, slice(None))
        windows(refs, c, 0, above)
        windows(refs, c, 280, below)
        for ref, at in refs:
            ref[at, c, 288:328, :] = jnp.zeros((40, 128), jnp.float32)

        def part(k, carry, c=c):
            r = pl.multiple_of(k * 32, 32)
            windows(refs, c, RIM + r, slide[c, pl.ds(r, 32), :].astype(jnp.float32))
            return carry

        lax.fori_loop(0, 8, part, 0)
    for b, (ref, at) in enumerate(refs):
        patch_rows(ref, at, lhs1, b)

    def first(n, carry):
        lanes = pl.ds(pl.multiple_of(n * 256, 256), 256)
        acc = gelu(jnp.dot(lhs1[...], toep[:, lanes], preferred_element_type=jnp.float32))
        for b in range(BLOCKS):
            for u in range(2):
                fmap[b, 2 * n + u, 0:ROWS1, :] = acc[ROWS1 * b : ROWS1 * b + ROWS1, 128 * u : 128 * u + 128]
        return carry

    lax.fori_loop(0, BLOCK_LANES // 256, first, 0)


def stem_kernel(
    ca_ref, cb_ref, edge_in, fmap_in, toep, w2, w3, wk, wv,
    edge, fmap, kv,
    lhs1, lhs2, smap, lhs3, third,
    *, col_last, row_last,
):
    col = lax.axis_index("cols")
    row = lax.axis_index("rows")
    even_col = col % 2 == 0
    lane = lanes_of((STRIP, 128))
    ca = ca_ref[...].astype(jnp.float32)
    cb = cb_ref[...].astype(jnp.float32)
    left_all = jnp.where(even_col, cb, ca)
    right_all = jnp.where(even_col, ca, cb)
    at_right = 512 + BEFORE - 4 * BLOCK_COLS * (BLOCKS - 1)
    for c in range(3):
        for half in range(2):
            g = BEFORE * (2 * c + half)
            rows = slice(half * STRIP, half * STRIP + STRIP)
            left = pltpu.roll(left_all, 128 - g, 1) if g else left_all
            right = pltpu.roll(right_all, (at_right - g) % 128, 1)
            edge[0, c, rows, :] = jnp.where(lane < BEFORE, left, edge_in[0, c, rows, :])
            edge[1, c, rows, :] = jnp.where(
                (lane >= at_right) & (lane < at_right + AFTER), right, edge_in[1, c, rows, :]
            )
    patch_rows(edge, 0, lhs1, 0)
    patch_rows(edge, 1, lhs1, 1)
    for slot, b, tiles in ((0, 0, (0, 1)), (1, BLOCKS - 1, (5,))):
        for n in tiles:
            acc = gelu(
                jnp.dot(
                    lhs1[ROWS1 * slot : ROWS1 * slot + ROWS1, :],
                    toep[:, 256 * n : 256 * n + 256],
                    preferred_element_type=jnp.float32,
                )
            )
            for u in range(2):
                fmap[b, 2 * n + u, 0:ROWS1, :] = acc[:, 128 * u : 128 * u + 128]

    @pl.when(row == 0)
    def _():
        for b in range(BLOCKS):
            fmap[b, :, 0:5, :] = jnp.zeros((BLOCK_LANES // 128, 5, 128), jnp.float32)

    @pl.when(row == row_last)
    def _():
        for b in range(BLOCKS):
            fmap[b, :, 69:70, :] = jnp.zeros((BLOCK_LANES // 128, 1, 128), jnp.float32)

    @pl.when(col == 0)
    def _():
        fmap[0, 0:2, 0:ROWS1, :] = jnp.zeros((2, ROWS1, 128), jnp.float32)
        fmap[0, 2, 0:ROWS1, 0:64] = jnp.zeros((ROWS1, 64), jnp.float32)

    @pl.when(col == col_last)
    def _():
        tile, side = divmod(133 - 4 * BLOCK_COLS, 2)
        fmap[4, tile, 0:ROWS1, 64 * side : 64 * side + 64] = jnp.zeros((ROWS1, 64), jnp.float32)

    for kh in range(6):
        for pair in range(COLS2 // 2):
            both = []
            for j in (2 * pair, 2 * pair + 1):
                b, t = divmod(j, 7)
                rows = pl.ds(kh, ROWS2, stride=4)
                tiles = [divmod(14 * b + 2 * t + u, 14) for u in range(3)]
                both.append([fmap[block, tile, rows, :] for block, tile in tiles])
            for u in range(3):
                lhs2[48 * pair : 48 * pair + 48, 384 * kh + 128 * u : 384 * kh + 128 * u + 128] = jnp.concatenate(
                    [both[0][u], both[1][u]], axis=0
                ).astype(jnp.bfloat16)
    for start, size in ((0, 288), (288, 288), (576, 240)):
        acc = gelu(jnp.dot(lhs2[start : start + size, :], w2[...], preferred_element_type=jnp.float32))
        for u in range(2):
            smap[u, start // ROWS2 : (start + size) // ROWS2] = acc[:, 128 * u : 128 * u + 128].reshape(
                size // ROWS2, ROWS2, 128
            )

    @pl.when(row == 0)
    def _():
        smap[:, :, 0:1, :] = jnp.zeros((2, COLS2, 1, 128), jnp.float32)

    @pl.when(col == 0)
    def _():
        smap[:, 0] = jnp.zeros((2, ROWS2, 128), jnp.float32)

    for kh in range(3):
        for kw in range(3):
            k = 3 * kh + kw
            for pair in range(8):
                for u in range(2):
                    lhs3[16 * pair : 16 * pair + 16, 256 * k + 128 * u : 256 * k + 128 * u + 128] = jnp.concatenate(
                        [
                            smap[u, 4 * pair + 2 * v + kw, pl.ds(kh, 8, stride=2), :]
                            for v in range(2)
                        ],
                        axis=0,
                    ).astype(jnp.bfloat16)

    def conv3(n, carry):
        lanes = pl.ds(pl.multiple_of(n * 256, 256), 256)
        third[:, lanes] = jnp.dot(lhs3[...], w3[:, lanes], preferred_element_type=jnp.float32)
        return carry

    lax.fori_loop(0, 4, conv3, 0)
    tokens = third[...]
    centred = tokens - jnp.mean(tokens, axis=-1, keepdims=True)
    var = jnp.mean(centred * centred, axis=-1, keepdims=True)
    lhs3[:, 0:1024] = (centred * lax.rsqrt(var + 1e-05)).astype(jnp.bfloat16)

    def project(n, carry):
        start = pl.multiple_of(n * 256, 256)
        for i, w in enumerate((wk, wv)):
            rows = jnp.dot(lhs3[:, 0:1024], w[:, pl.ds(start, 256)], preferred_element_type=jnp.float32)
            kv[:, pl.ds(1024 * i + start, 256)] = rows.astype(jnp.bfloat16)
        return carry

    lax.fori_loop(0, 4, project, 0)


def attend_kernel(q, mine, theirs, out, *, bit_of, keep):
    n = out.shape[0]
    quarter = 2 * (lax.axis_index("rows") % 2) + (bit_of() if keep else 1 - bit_of())
    rows = pl.ds(pl.multiple_of(quarter * n, n), n)
    scale = 1.0 / math.sqrt(128)
    lane = lanes_of((n, 128))
    stat = jnp.zeros((n, 128), jnp.float32)
    for h in range(HEADS):
        lanes = slice(128 * h, 128 * h + 128)
        past = slice(1024 + 128 * h, 1024 + 128 * h + 128)
        keys = jnp.concatenate([mine[:, lanes], theirs[:, lanes]], axis=0)
        values = jnp.concatenate([mine[:, past], theirs[:, past]], axis=0)
        scores = lax.dot_general(
            q[rows, lanes], keys, (((1,), (1,)), ((), ())), preferred_element_type=jnp.float32
        ) * scale
        peak = jnp.max(scores, axis=1, keepdims=True)
        w = jnp.exp(scores - peak)
        total = jnp.sum(w, axis=1, keepdims=True)
        o = jnp.dot(w.astype(jnp.bfloat16), values, preferred_element_type=jnp.float32)
        out[:, lanes] = (o * (1.0 / total)).astype(out.dtype)
        stat = jnp.where(lane == h, peak + jnp.log(total), stat)
    out[:, 1024:1152] = stat if keep else pack_stat(stat)


def pack_stat(stat):
    lane = lanes_of(stat.shape)
    stat = jnp.where(lane < HEADS, stat, 0.0)
    high = stat.astype(jnp.bfloat16).astype(jnp.float32)
    rest = stat - high
    mid = rest.astype(jnp.bfloat16).astype(jnp.float32)
    low = rest - mid
    return (high + pltpu.roll(mid, HEADS, 1) + pltpu.roll(low, 2 * HEADS, 1)).astype(jnp.bfloat16)


def unpack_stat(stat):
    stat = stat.astype(jnp.float32)
    return stat + pltpu.roll(stat, 128 - HEADS, 1) + pltpu.roll(stat, 128 - 2 * HEADS, 1)


def merge_kernel(keep_ref, recv_ref, *outs, bit_of):
    n = keep_ref.shape[0]
    mine = keep_ref[:, 1024:1152]
    theirs = unpack_stat(recv_ref[:, 1024:1152])
    peak = jnp.maximum(mine, theirs)
    em = jnp.exp(mine - peak)
    total = em + jnp.exp(theirs - peak)
    share = em / total
    stat = peak + jnp.log(total)
    merged = []
    for h in range(HEADS):
        lanes = slice(128 * h, 128 * h + 128)
        a = keep_ref[:, lanes]
        b = recv_ref[:, lanes].astype(jnp.float32)
        merged.append(b + jnp.broadcast_to(share[:, h : h + 1], (n, 128)) * (a - b))
    if bit_of is None:
        for h in range(HEADS):
            outs[0][:, 128 * h : 128 * h + 128] = merged[h].astype(jnp.bfloat16)
        return
    upper = bit_of() == 1
    half = n // 2
    for h in range(HEADS):
        lanes = slice(128 * h, 128 * h + 128)
        outs[0][:, lanes] = jnp.where(upper, merged[h][half:], merged[h][:half])
        outs[1][:, lanes] = jnp.where(upper, merged[h][:half], merged[h][half:]).astype(jnp.bfloat16)
    outs[0][:, 1024:1152] = jnp.where(upper, stat[half:], stat[:half])
    outs[1][:, 1024:1152] = pack_stat(jnp.where(upper, stat[:half], stat[half:]))


def near(x):
    return pltpu.with_memory_space_constraint(x, VMEM)


def call(kernel, name, args, outs, scratch=(), aliases=None, flops=0, moved=0, limit=None):
    spec = pl.BlockSpec(memory_space=VMEM)
    return pl.pallas_call(
        kernel,
        in_specs=[spec] * len(args),
        out_specs=[spec] * len(outs),
        out_shape=tuple(outs),
        scratch_shapes=list(scratch),
        input_output_aliases=aliases or {},
        cost_estimate=pl.CostEstimate(flops=flops, bytes_accessed=moved, transcendentals=0),
        compiler_params=pltpu.CompilerParams(vmem_limit_bytes=limit),
        name=name,
    )(*[near(x) for x in args])


def merge(keep, recv, bit_of):
    n, width = keep.shape
    if bit_of is None:
        outs = (jax.ShapeDtypeStruct((n, 1024), jnp.bfloat16),)
    else:
        outs = (VMEM((n // 2, width), jnp.float32), VMEM((n // 2, width), jnp.bfloat16))
    out = call(functools.partial(merge_kernel, bit_of=bit_of), "merge", (keep, recv), outs, limit=8 << 20)
    return out[0] if bit_of is None else out


def swap_pairs(size, odd):
    pairs = []
    for i in range(1 if odd else 0, size - 1, 2):
        pairs += [(i, i + 1), (i + 1, i)]
    return pairs


def bits_of(size):
    return size.bit_length() - 1


def plan(mesh):
    n_rows, n_cols = mesh.shape["rows"], mesh.shape["cols"]
    row_bits = [("rows", k) for k in range(1, bits_of(n_rows))]
    col_bits = [("cols", k) for k in range(bits_of(n_cols))]
    return row_bits + col_bits, col_bits[:1] + row_bits + col_bits[1:]


def solution(mesh):
    n_rows, n_cols = mesh.shape["rows"], mesh.shape["cols"]
    orders = plan(mesh)

    def partner(index, stage):
        col, row = divmod(index, n_rows)
        axis, k = orders[row & 1][stage]
        return col * n_rows + (row ^ (1 << k)) if axis == "rows" else (col ^ (1 << k)) * n_rows + row

    def exchange(value, stage):
        pairs = [(i, partner(i, stage)) for i in range(n_rows * n_cols)]
        return lax.ppermute(value, ("cols", "rows"), pairs)

    def bit_of(stage):
        def read():
            row = lax.axis_index("rows")
            (axis0, k0), (axis1, k1) = orders[0][stage], orders[1][stage]
            return jnp.where(
                row % 2 == 0, (lax.axis_index(axis0) >> k0) & 1, (lax.axis_index(axis1) >> k1) & 1
            )

        return read

    def order_queries(queries):
        latents, width = queries.shape
        share = latents // (n_rows * n_cols)
        names = [("cols", k) for k in reversed(range(bits_of(n_cols)))]
        names += [("rows", k) for k in reversed(range(bits_of(n_rows)))]
        split = queries.reshape([2] * len(names) + [share, width])
        at = names.index(("rows", 0))
        rest = names[:at] + names[at + 1 :]
        halves = []
        for core in range(2):
            part = lax.index_in_dim(split, core, at, keepdims=False)
            axes = [rest.index(name) for name in orders[core]]
            halves.append(part.transpose(axes + [len(rest), len(rest) + 1]).reshape(latents // 2, width))
        return jnp.concatenate(halves, axis=0)

    def on_device(slide_pixels, stem_first, stem_second, stem_third, key_weight, value_weight, queries):
        bf16, f32 = jnp.bfloat16, jnp.float32
        rim = VMEM((3, RIM, 512), bf16)
        row_a, row_b = call(row_edges_kernel, "row_edges", (slide_pixels,), (rim, rim), limit=8 << 20)
        row_a = lax.ppermute(row_a, "rows", swap_pairs(n_rows, False))
        row_b = lax.ppermute(row_b, "rows", swap_pairs(n_rows, True))
        strip = VMEM((STRIP, 128), bf16)
        col_a, col_b = call(
            col_edges_kernel, "col_edges", (slide_pixels, row_a, row_b), (strip, strip), limit=8 << 20
        )
        col_a = lax.ppermute(col_a, "cols", swap_pairs(n_cols, False))
        col_b = lax.ppermute(col_b, "cols", swap_pairs(n_cols, True))

        taps = stem_first.transpose(2, 0, 1, 3).reshape(TAPS1, 6, 64)
        taps = sum(
            jnp.pad(taps, ((0, 0), (top, 42 - top), (64 * side, 64 - 64 * side)))
            for top, side in ((0, 0), (4, 1), (24, 0), (28, 1))
        )
        (toep,) = call(
            band_kernel, "band", (taps,), (VMEM((TAPS1 * 128, BLOCK_LANES), bf16),), moved=4 << 20, limit=2 << 20
        )
        edge_shape = VMEM((2, 3, 328, 128), f32)
        fmap_shape = VMEM((BLOCKS, BLOCK_LANES // 128, 104, 128), f32)
        edge, fmap = call(
            inner_kernel,
            "inner",
            (slide_pixels, row_a, row_b, toep),
            (edge_shape, fmap_shape),
            scratch=[pltpu.VMEM((3, 3, 328, 128), f32), pltpu.VMEM((BLOCKS * ROWS1, TAPS1 * 128), bf16)],
            flops=2 * BLOCKS * ROWS1 * TAPS1 * 128 * BLOCK_LANES,
            moved=16 << 20,
            limit=16 << 20,
        )
        _, _, kv = call(
            functools.partial(stem_kernel, col_last=n_cols - 1, row_last=n_rows - 1),
            "stem",
            (
                col_a, col_b, edge, fmap, toep,
                stem_second.reshape(2304, 256), stem_third.reshape(2304, 1024), key_weight, value_weight,
            ),
            (edge_shape, fmap_shape, VMEM((128, 2048), bf16)),
            scratch=[
                pltpu.VMEM((2 * ROWS1, TAPS1 * 128), bf16),
                pltpu.VMEM((COLS2 * ROWS2, 2304), bf16),
                pltpu.VMEM((2, COLS2, ROWS2, 128), f32),
                pltpu.VMEM((128, 2304), bf16),
                pltpu.VMEM((128, 1024), f32),
            ],
            aliases={2: 0, 3: 1},
            flops=3 << 30,
            limit=16 << 20,
        )
        kv_other = lax.ppermute(kv, "rows", swap_pairs(n_rows, False))
        ordered = order_queries(queries)
        quarter = queries.shape[0] // 4
        width = 1024 + STAT

        def attend(q, keep, dtype):
            return call(
                functools.partial(attend_kernel, bit_of=bit_of(0), keep=keep),
                "attend",
                (q, kv, kv_other),
                (VMEM((quarter, width), dtype),),
                flops=1 << 30,
                limit=8 << 20,
            )[0]

        send = attend(ordered, False, bf16)
        ordered, send = lax.optimization_barrier((ordered, send))
        recv = exchange(send, 0)
        keep = attend(ordered, True, f32)
        for stage in range(1, len(orders[0])):
            keep, send = merge(keep, recv, bit_of(stage))
            recv = exchange(send, stage)
        return merge(keep, recv, None)

    placed = (P(None, "rows", "cols"), P(), P(), P(), P(), P(), P())
    return jax.shard_map(
        on_device, mesh=mesh, in_specs=placed, out_specs=P(("cols", "rows"), None), check_vma=False
    )
```

```python
import functools
import math

import jax
import jax.numpy as jnp
from jax import lax
from jax.experimental import pallas as pl
from jax.experimental.pallas import tpu as pltpu
from jax.sharding import PartitionSpec as P

HEADS = 8
BEFORE, AFTER = 21, 5
TAPS1 = 18
BLOCK_COLS = 28
BLOCKS = 5
BLOCK_LANES = BLOCK_COLS * 64
ROWS1 = 80
ROWS2 = 24
COLS2 = 34
STAT = 128
RIM = 24
EDGE, MID = 16, 48
ROWS_ALL = (MID + EDGE) * 5 + 48
STRIP = 144
VMEM = pltpu.MemorySpace.VMEM


def gelu(x):
    inner = x * (0.7978845608028654 + 0.035677408136300125 * (x * x))
    half = 0.5 * x
    return half + half * jnp.tanh(inner)


def lanes_of(shape):
    return lax.broadcasted_iota(jnp.int32, shape, len(shape) - 1)


def row_edges_kernel(slide_hbm, a_ref, b_ref, sems):
    even = lax.axis_index("rows") % 2 == 0
    height = slide_hbm.shape[1]

    def send(first, second):
        copies = [
            pltpu.make_async_copy(slide_hbm.at[:, pl.ds(height - RIM, RIM), :], first, sems.at[0]),
            pltpu.make_async_copy(slide_hbm.at[:, pl.ds(0, RIM), :], second, sems.at[1]),
        ]
        for copy in copies:
            copy.start()
        for copy in copies:
            copy.wait()

    @pl.when(even)
    def _():
        send(a_ref, b_ref)

    @pl.when(jnp.logical_not(even))
    def _():
        send(b_ref, a_ref)


def rims(c, ra_ref, rb_ref, lanes):
    even = lax.axis_index("rows") % 2 == 0
    ra = ra_ref[c, :, lanes].astype(jnp.float32)
    rb = rb_ref[c, :, lanes].astype(jnp.float32)
    return jnp.where(even, rb, ra), jnp.where(even, ra, rb)[0:8]


def col_edges_kernel(slide, ra_ref, rb_ref, a_ref, b_ref):
    even = lax.axis_index("cols") % 2 == 0
    lane = lanes_of((STRIP, 128))
    first = jnp.zeros((STRIP, 128), jnp.float32)
    last = jnp.zeros((STRIP, 128), jnp.float32)
    for c in range(3):
        sides = []
        for lanes in (slice(0, 128), slice(384, 512)):
            above, below = rims(c, ra_ref, rb_ref, lanes)
            sides.append(jnp.concatenate([above, slide[c, :, lanes].astype(jnp.float32), below], axis=0))
        for half in range(2):
            g = BEFORE * (2 * c + half)
            rows = slice(half * STRIP, half * STRIP + STRIP)
            lo = pltpu.roll(sides[0][rows], g, 1) if g else sides[0][rows]
            hi = pltpu.roll(sides[1][rows], (g + BEFORE) % 128, 1)
            first = jnp.where((lane >= g) & (lane < g + AFTER), lo, first)
            last = jnp.where((lane >= g) & (lane < g + BEFORE), hi, last)
    a_ref[...] = jnp.where(even, last, first).astype(jnp.bfloat16)
    b_ref[...] = jnp.where(even, first, last).astype(jnp.bfloat16)


def band_kernel(taps_ref, toep):
    def band(k, carry):
        base = pl.multiple_of(k * 128, 128)
        toep[pl.ds(base, 128), :] = jnp.zeros((128, BLOCK_LANES), jnp.bfloat16)
        p0 = taps_ref[k, 0:16, :]
        p1 = taps_ref[k, 16:32, :]
        p2 = taps_ref[k, 32:48, :]
        for m in range(BLOCK_LANES // 256):
            toep[pl.ds(base + 16 * m, 16), 256 * m : 256 * m + 128] = p0
            toep[pl.ds(base + 16 * m, 16), 256 * m + 128 : 256 * m + 256] = p1
            toep[pl.ds(base + 16 * m + 16, 16), 256 * m + 128 : 256 * m + 256] = p2
        return carry

    lax.fori_loop(0, TAPS1, band, 0)


def picks(first):
    lane = lax.broadcasted_iota(jnp.int32, (256, 128), 1)
    source = lax.broadcasted_iota(jnp.int32, (256, 128), 0)
    out = []
    for b, start in zip(range(BLOCKS), (0, 0, 128, 256, 256)):
        if b in first:
            hit = source + start == lane + (4 * BLOCK_COLS * b - BEFORE)
            out.append(jnp.where(hit, 1.0, 0.0).astype(jnp.bfloat16))
    return jnp.concatenate(out, axis=1)


def cut(rows):
    parts = []
    for blocks, start in (((0, 1), 0), ((2,), 128), ((3, 4), 256)):
        moved = jnp.dot(rows[:, start : start + 256], picks(blocks), preferred_element_type=jnp.float32)
        parts += [moved[:, 128 * i : 128 * i + 128] for i in range(len(blocks))]
    return parts


def window_kernel(slide, xb, lhs1):
    for c in range(3):
        for b, part in enumerate(cut(slide[c])):
            xb[b, c, RIM : RIM + 256, :] = part
    for b in range(BLOCKS):
        for c in range(3):
            for kh in range(6):
                k = 6 * c + kh
                lhs1[MID * b : MID * b + MID, 128 * k : 128 * k + 128] = xb[
                    b, c, pl.ds(RIM - BEFORE + kh + 4 * EDGE, MID, stride=4), :
                ].astype(jnp.bfloat16)


def patch_rows(ref, at, lhs1, slot):
    for c in range(3):
        for kh in range(6):
            k = 6 * c + kh
            lhs1[ROWS1 * slot : ROWS1 * slot + ROWS1, 128 * k : 128 * k + 128] = ref[
                at, c, pl.ds(RIM - BEFORE + kh, ROWS1, stride=4), :
            ].astype(jnp.bfloat16)


def inner_kernel(ra_ref, rb_ref, toep, xb_in, lhs1_in, xb, fmap, lhs1):
    outer = []
    for c in range(3):
        outer += rims(c, ra_ref, rb_ref, slice(None))
    parts = cut(jnp.concatenate(outer, axis=0).astype(jnp.bfloat16))
    for b in range(BLOCKS):
        for c in range(3):
            xb[b, c, 0:RIM, :] = parts[b][32 * c : 32 * c + RIM]
            xb[b, c, 280:288, :] = parts[b][32 * c + RIM : 32 * c + 32]
            xb[b, c, 288:328, :] = jnp.zeros((40, 128), jnp.float32)
    top, bottom = MID * BLOCKS, (MID + EDGE) * BLOCKS
    for c in range(3):
        for kh in range(6):
            lanes = slice(128 * (6 * c + kh), 128 * (6 * c + kh) + 128)
            low = []
            for b in range(BLOCKS):
                lhs1[top + EDGE * b : top + EDGE * b + EDGE, lanes] = xb[
                    b, c, pl.ds(RIM - BEFORE + kh, EDGE, stride=4), :
                ].astype(jnp.bfloat16)
                low.append(xb[b, c, pl.ds(RIM - BEFORE + kh + 4 * (EDGE + MID), 8, stride=4), :])
            low.append(jnp.zeros((8, 128), jnp.float32))
            lhs1[bottom : bottom + 48, lanes] = jnp.concatenate(low, axis=0).astype(jnp.bfloat16)
    for n in range(BLOCK_LANES // 256):
        acc = gelu(jnp.dot(lhs1[...], toep[:, 256 * n : 256 * n + 256], preferred_element_type=jnp.float32))
        for b in range(BLOCKS):
            for u in range(2):
                half = slice(128 * u, 128 * u + 128)
                fmap[b, 2 * n + u, 0:EDGE, :] = acc[top + EDGE * b : top + EDGE * b + EDGE, half]
                fmap[b, 2 * n + u, EDGE : EDGE + MID, :] = acc[MID * b : MID * b + MID, half]
                fmap[b, 2 * n + u, EDGE + MID : EDGE + MID + 8, :] = acc[bottom + 8 * b : bottom + 8 * b + 8, half]


def stem_kernel(
    ca_ref, cb_ref, xb_in, fmap_in, toep, w2, w3, wk_far, wv_far,
    xb, fmap, normed, wk, wv,
    lhs1, lhs2, smap, lhs3, third, sems,
    *, col_last, row_last,
):
    copies = [pltpu.make_async_copy(wk_far, wk, sems.at[0]), pltpu.make_async_copy(wv_far, wv, sems.at[1])]
    for copy in copies:
        copy.start()
    col = lax.axis_index("cols")
    row = lax.axis_index("rows")
    even_col = col % 2 == 0
    lane = lanes_of((STRIP, 128))
    ca = ca_ref[...].astype(jnp.float32)
    cb = cb_ref[...].astype(jnp.float32)
    left_all = jnp.where(even_col, cb, ca)
    right_all = jnp.where(even_col, ca, cb)
    at_right = 512 + BEFORE - 4 * BLOCK_COLS * (BLOCKS - 1)
    for c in range(3):
        for half in range(2):
            g = BEFORE * (2 * c + half)
            rows = slice(half * STRIP, half * STRIP + STRIP)
            left = pltpu.roll(left_all, 128 - g, 1) if g else left_all
            right = pltpu.roll(right_all, (at_right - g) % 128, 1)
            xb[0, c, rows, :] = jnp.where(lane < BEFORE, left, xb[0, c, rows, :])
            xb[BLOCKS - 1, c, rows, :] = jnp.where(
                (lane >= at_right) & (lane < at_right + AFTER), right, xb[BLOCKS - 1, c, rows, :]
            )
    patch_rows(xb, 0, lhs1, 0)
    patch_rows(xb, BLOCKS - 1, lhs1, 1)
    for slot, b, tiles in ((0, 0, (0, 1)), (1, BLOCKS - 1, (5,))):
        for n in tiles:
            acc = gelu(
                jnp.dot(
                    lhs1[ROWS1 * slot : ROWS1 * slot + ROWS1, :],
                    toep[:, 256 * n : 256 * n + 256],
                    preferred_element_type=jnp.float32,
                )
            )
            for u in range(2):
                fmap[b, 2 * n + u, 0:ROWS1, :] = acc[:, 128 * u : 128 * u + 128]

    @pl.when(row == 0)
    def _():
        for b in range(BLOCKS):
            fmap[b, :, 0:5, :] = jnp.zeros((BLOCK_LANES // 128, 5, 128), jnp.float32)

    @pl.when(row == row_last)
    def _():
        for b in range(BLOCKS):
            fmap[b, :, 69:70, :] = jnp.zeros((BLOCK_LANES // 128, 1, 128), jnp.float32)

    @pl.when(col == 0)
    def _():
        fmap[0, 0:2, 0:ROWS1, :] = jnp.zeros((2, ROWS1, 128), jnp.float32)
        fmap[0, 2, 0:ROWS1, 0:64] = jnp.zeros((ROWS1, 64), jnp.float32)

    @pl.when(col == col_last)
    def _():
        tile, side = divmod(133 - 4 * BLOCK_COLS, 2)
        fmap[4, tile, 0:ROWS1, 64 * side : 64 * side + 64] = jnp.zeros((ROWS1, 64), jnp.float32)

    for kh in range(6):
        for pair in range(COLS2 // 2):
            both = []
            for j in (2 * pair, 2 * pair + 1):
                b, t = divmod(j, 7)
                rows = pl.ds(kh, ROWS2, stride=4)
                tiles = [divmod(14 * b + 2 * t + u, 14) for u in range(3)]
                both.append([fmap[block, tile, rows, :] for block, tile in tiles])
            for u in range(3):
                lhs2[48 * pair : 48 * pair + 48, 384 * kh + 128 * u : 384 * kh + 128 * u + 128] = jnp.concatenate(
                    [both[0][u], both[1][u]], axis=0
                ).astype(jnp.bfloat16)
    for start, size in ((0, 288), (288, 288), (576, 240)):
        acc = gelu(jnp.dot(lhs2[start : start + size, :], w2[...], preferred_element_type=jnp.float32))
        for u in range(2):
            smap[u, start // ROWS2 : (start + size) // ROWS2] = acc[:, 128 * u : 128 * u + 128].reshape(
                size // ROWS2, ROWS2, 128
            )

    @pl.when(row == 0)
    def _():
        smap[:, :, 0:1, :] = jnp.zeros((2, COLS2, 1, 128), jnp.float32)

    @pl.when(col == 0)
    def _():
        smap[:, 0] = jnp.zeros((2, ROWS2, 128), jnp.float32)

    for kh in range(3):
        for kw in range(3):
            k = 3 * kh + kw
            for pair in range(8):
                for u in range(2):
                    lhs3[16 * pair : 16 * pair + 16, 256 * k + 128 * u : 256 * k + 128 * u + 128] = jnp.concatenate(
                        [
                            smap[u, 4 * pair + 2 * v + kw, pl.ds(kh, 8, stride=2), :]
                            for v in range(2)
                        ],
                        axis=0,
                    ).astype(jnp.bfloat16)

    for n in range(4):
        lanes = slice(256 * n, 256 * n + 256)
        third[:, lanes] = jnp.dot(lhs3[...], w3[:, lanes], preferred_element_type=jnp.float32)
    tokens = third[...]
    centred = tokens - jnp.mean(tokens, axis=-1, keepdims=True)
    var = jnp.mean(centred * centred, axis=-1, keepdims=True)
    normed[...] = (centred * lax.rsqrt(var + 1e-05)).astype(jnp.bfloat16)
    for copy in copies:
        copy.wait()


def project_kernel(mine, theirs, wk, wv, kv, tokens):
    half = mine.shape[0]
    tokens[0:half] = mine[...]
    tokens[half:] = theirs[...]
    for i, w in enumerate((wk, wv)):
        for n in range(4):
            rows = jnp.dot(tokens[...], w[:, 256 * n : 256 * n + 256], preferred_element_type=jnp.float32)
            kv[:, 1024 * i + 256 * n : 1024 * i + 256 * n + 256] = rows.astype(jnp.bfloat16)


def attend_kernel(q, kv, out, *, bit_of, keep):
    n = out.shape[0]
    quarter = 2 * (lax.axis_index("rows") % 2) + (bit_of() if keep else 1 - bit_of())
    rows = pl.ds(pl.multiple_of(quarter * n, n), n)
    scale = 1.0 / math.sqrt(128)
    lane = lanes_of((n, 128))
    stat = jnp.zeros((n, 128), jnp.float32)
    for h in range(HEADS):
        lanes = slice(128 * h, 128 * h + 128)
        past = slice(1024 + 128 * h, 1024 + 128 * h + 128)
        scores = lax.dot_general(
            q[rows, lanes], kv[:, lanes], (((1,), (1,)), ((), ())), preferred_element_type=jnp.float32
        ) * scale
        peak = jnp.max(scores, axis=1, keepdims=True)
        w = jnp.exp(scores - peak)
        total = jnp.sum(w, axis=1, keepdims=True)
        o = jnp.dot(w.astype(jnp.bfloat16), kv[:, past], preferred_element_type=jnp.float32)
        out[:, lanes] = (o * (1.0 / total)).astype(out.dtype)
        stat = jnp.where(lane == h, peak + jnp.log(total), stat)
    out[:, 1024:1152] = stat if keep else pack_stat(stat)


def pack_stat(stat):
    lane = lanes_of(stat.shape)
    stat = jnp.where(lane < HEADS, stat, 0.0)
    high = stat.astype(jnp.bfloat16).astype(jnp.float32)
    rest = stat - high
    mid = rest.astype(jnp.bfloat16).astype(jnp.float32)
    low = rest - mid
    return (high + pltpu.roll(mid, HEADS, 1) + pltpu.roll(low, 2 * HEADS, 1)).astype(jnp.bfloat16)


def unpack_stat(stat):
    stat = stat.astype(jnp.float32)
    return stat + pltpu.roll(stat, 128 - HEADS, 1) + pltpu.roll(stat, 128 - 2 * HEADS, 1)


def merge_kernel(keep_ref, recv_ref, *outs, bit_of):
    n = keep_ref.shape[0]
    mine = keep_ref[:, 1024:1152]
    theirs = unpack_stat(recv_ref[:, 1024:1152])
    peak = jnp.maximum(mine, theirs)
    em = jnp.exp(mine - peak)
    total = em + jnp.exp(theirs - peak)
    share = em / total
    stat = peak + jnp.log(total)
    merged = []
    for h in range(HEADS):
        lanes = slice(128 * h, 128 * h + 128)
        a = keep_ref[:, lanes]
        b = recv_ref[:, lanes].astype(jnp.float32)
        merged.append(b + jnp.broadcast_to(share[:, h : h + 1], (n, 128)) * (a - b))
    if bit_of is None:
        for h in range(HEADS):
            outs[0][:, 128 * h : 128 * h + 128] = merged[h].astype(jnp.bfloat16)
        return
    upper = bit_of() == 1
    half = n // 2
    for h in range(HEADS):
        lanes = slice(128 * h, 128 * h + 128)
        outs[0][:, lanes] = jnp.where(upper, merged[h][half:], merged[h][:half])
        outs[1][:, lanes] = jnp.where(upper, merged[h][:half], merged[h][half:]).astype(jnp.bfloat16)
    outs[0][:, 1024:1152] = jnp.where(upper, stat[half:], stat[:half])
    outs[1][:, 1024:1152] = pack_stat(jnp.where(upper, stat[:half], stat[half:]))


def call(kernel, name, args, outs, scratch=(), aliases=None, flops=0, moved=0, limit=None, far=()):
    spec = pl.BlockSpec(memory_space=VMEM)
    far_spec = pl.BlockSpec(memory_space=pltpu.HBM)
    return pl.pallas_call(
        kernel,
        in_specs=[far_spec if i in far else spec for i in range(len(args))],
        out_specs=[spec] * len(outs),
        out_shape=tuple(outs),
        scratch_shapes=list(scratch),
        input_output_aliases=aliases or {},
        cost_estimate=pl.CostEstimate(flops=flops, bytes_accessed=moved, transcendentals=0),
        compiler_params=pltpu.CompilerParams(vmem_limit_bytes=limit),
        name=name,
    )(*[pltpu.with_memory_space_constraint(x, pltpu.HBM if i in far else VMEM) for i, x in enumerate(args)])


def merge(keep, recv, bit_of):
    n, width = keep.shape
    if bit_of is None:
        outs = (jax.ShapeDtypeStruct((n, 1024), jnp.bfloat16),)
    else:
        outs = (VMEM((n // 2, width), jnp.float32), VMEM((n // 2, width), jnp.bfloat16))
    out = call(functools.partial(merge_kernel, bit_of=bit_of), "merge", (keep, recv), outs, limit=8 << 20)
    return out[0] if bit_of is None else out


def swap_pairs(size, odd):
    pairs = []
    for i in range(1 if odd else 0, size - 1, 2):
        pairs += [(i, i + 1), (i + 1, i)]
    return pairs


def bits_of(size):
    return size.bit_length() - 1


def plan(mesh):
    n_rows, n_cols = mesh.shape["rows"], mesh.shape["cols"]
    row_bits = [("rows", k) for k in range(1, bits_of(n_rows))]
    col_bits = [("cols", k) for k in range(bits_of(n_cols))]
    return row_bits + col_bits, col_bits[:1] + row_bits + col_bits[1:]


def solution(mesh):
    n_rows, n_cols = mesh.shape["rows"], mesh.shape["cols"]
    orders = plan(mesh)

    def partner(index, stage):
        col, row = divmod(index, n_rows)
        axis, k = orders[row & 1][stage]
        return col * n_rows + (row ^ (1 << k)) if axis == "rows" else (col ^ (1 << k)) * n_rows + row

    def exchange(value, stage):
        pairs = [(i, partner(i, stage)) for i in range(n_rows * n_cols)]
        return lax.ppermute(value, ("cols", "rows"), pairs)

    def bit_of(stage):
        def read():
            row = lax.axis_index("rows")
            (axis0, k0), (axis1, k1) = orders[0][stage], orders[1][stage]
            return jnp.where(
                row % 2 == 0, (lax.axis_index(axis0) >> k0) & 1, (lax.axis_index(axis1) >> k1) & 1
            )

        return read

    def order_queries(queries):
        latents, width = queries.shape
        share = latents // (n_rows * n_cols)
        names = [("cols", k) for k in reversed(range(bits_of(n_cols)))]
        names += [("rows", k) for k in reversed(range(bits_of(n_rows)))]
        split = queries.reshape([2] * len(names) + [share, width])
        at = names.index(("rows", 0))
        rest = names[:at] + names[at + 1 :]
        halves = []
        for core in range(2):
            part = lax.index_in_dim(split, core, at, keepdims=False)
            axes = [rest.index(name) for name in orders[core]]
            halves.append(part.transpose(axes + [len(rest), len(rest) + 1]).reshape(latents // 2, width))
        return jnp.concatenate(halves, axis=0)

    def on_device(slide_pixels, stem_first, stem_second, stem_third, key_weight, value_weight, queries):
        bf16, f32 = jnp.bfloat16, jnp.float32
        rim = VMEM((3, RIM, 512), bf16)
        row_a, row_b = call(
            row_edges_kernel,
            "row_edges",
            (slide_pixels,),
            (rim, rim),
            scratch=[pltpu.SemaphoreType.DMA((2,))],
            limit=8 << 20,
            far=(0,),
        )
        row_a = lax.ppermute(row_a, "rows", swap_pairs(n_rows, False))
        row_b = lax.ppermute(row_b, "rows", swap_pairs(n_rows, True))
        strip = VMEM((STRIP, 128), bf16)
        col_a, col_b = call(
            col_edges_kernel, "col_edges", (slide_pixels, row_a, row_b), (strip, strip), limit=8 << 20
        )
        col_a = lax.ppermute(col_a, "cols", swap_pairs(n_cols, False))
        col_b = lax.ppermute(col_b, "cols", swap_pairs(n_cols, True))

        taps = stem_first.transpose(2, 0, 1, 3).reshape(TAPS1, 6, 64)
        taps = sum(
            jnp.pad(taps, ((0, 0), (top, 42 - top), (64 * side, 64 - 64 * side)))
            for top, side in ((0, 0), (4, 1), (24, 0), (28, 1))
        )
        (toep,) = call(
            band_kernel, "band", (taps,), (VMEM((TAPS1 * 128, BLOCK_LANES), bf16),), moved=4 << 20, limit=2 << 20
        )
        xb_shape = VMEM((BLOCKS, 3, 328, 128), f32)
        lhs1_shape = VMEM((ROWS_ALL, TAPS1 * 128), bf16)
        fmap_shape = VMEM((BLOCKS, BLOCK_LANES // 128, 104, 128), f32)
        xb, lhs1 = call(
            window_kernel, "windows", (slide_pixels,), (xb_shape, lhs1_shape), flops=1 << 28, moved=4 << 20, limit=8 << 20
        )
        xb, fmap, _ = call(
            inner_kernel,
            "inner",
            (row_a, row_b, toep, xb, lhs1),
            (xb_shape, fmap_shape, lhs1_shape),
            aliases={3: 0, 4: 2},
            flops=2 * ROWS_ALL * TAPS1 * 128 * BLOCK_LANES,
            moved=16 << 20,
            limit=8 << 20,
        )
        _, _, normed, key_near, value_near = call(
            functools.partial(stem_kernel, col_last=n_cols - 1, row_last=n_rows - 1),
            "stem",
            (
                col_a, col_b, xb, fmap, toep, stem_second.reshape(2304, 256), stem_third.reshape(2304, 1024),
                key_weight, value_weight,
            ),
            (xb_shape, fmap_shape, VMEM((128, 1024), bf16), VMEM((1024, 1024), bf16), VMEM((1024, 1024), bf16)),
            scratch=[
                pltpu.VMEM((2 * ROWS1, TAPS1 * 128), bf16),
                pltpu.VMEM((COLS2 * ROWS2, 2304), bf16),
                pltpu.VMEM((2, COLS2, ROWS2, 128), f32),
                pltpu.VMEM((128, 2304), bf16),
                pltpu.VMEM((128, 1024), f32),
                pltpu.SemaphoreType.DMA((2,)),
            ],
            aliases={2: 0, 3: 1},
            far=(7, 8),
            flops=3 << 30,
            limit=16 << 20,
        )
        normed_other = lax.ppermute(normed, "rows", swap_pairs(n_rows, False))
        (kv,) = call(
            project_kernel,
            "project",
            (normed, normed_other, key_near, value_near),
            (VMEM((256, 2048), bf16),),
            scratch=[pltpu.VMEM((256, 1024), bf16)],
            flops=1 << 30,
            limit=8 << 20,
        )
        ordered = order_queries(queries)
        quarter = queries.shape[0] // 4
        width = 1024 + STAT

        def attend(q, keep, dtype):
            return call(
                functools.partial(attend_kernel, bit_of=bit_of(0), keep=keep),
                "attend",
                (q, kv),
                (VMEM((quarter, width), dtype),),
                flops=1 << 30,
                limit=8 << 20,
            )[0]

        send = attend(ordered, False, bf16)
        ordered, send = lax.optimization_barrier((ordered, send))
        recv = exchange(send, 0)
        keep = attend(ordered, True, f32)
        for stage in range(1, len(orders[0])):
            keep, send = merge(keep, recv, bit_of(stage))
            recv = exchange(send, stage)
        return merge(keep, recv, None)

    placed = (P(None, "rows", "cols"), P(), P(), P(), P(), P(), P())
    return jax.shard_map(
        on_device, mesh=mesh, in_specs=placed, out_specs=P(("cols", "rows"), None), check_vma=False
    )
```

```python
import functools
import math

import jax
import jax.numpy as jnp
from jax import lax
from jax.experimental import pallas as pl
from jax.experimental.pallas import tpu as pltpu
from jax.sharding import PartitionSpec as P

HEADS = 8
BEFORE, AFTER = 21, 5
TAPS1 = 18
BLOCK_COLS = 28
BLOCKS = 5
BLOCK_LANES = BLOCK_COLS * 64
ROWS1 = 80
ROWS2 = 24
COLS2 = 34
STAT = 128
RIM = 24
EDGE, MID = 16, 48
ROWS_ALL = (MID + EDGE) * 5 + 48
STRIP = 144
VMEM = pltpu.MemorySpace.VMEM


def gelu(x):
    inner = x * (0.7978845608028654 + 0.035677408136300125 * (x * x))
    half = 0.5 * x
    return half + half * jnp.tanh(inner)


def lanes_of(shape):
    return lax.broadcasted_iota(jnp.int32, shape, len(shape) - 1)


def row_edges_kernel(slide_hbm, a_ref, b_ref, sems):
    even = lax.axis_index("rows") % 2 == 0
    height = slide_hbm.shape[1]

    def send(first, second):
        copies = [
            pltpu.make_async_copy(slide_hbm.at[:, pl.ds(height - RIM, RIM), :], first, sems.at[0]),
            pltpu.make_async_copy(slide_hbm.at[:, pl.ds(0, RIM), :], second, sems.at[1]),
        ]
        for copy in copies:
            copy.start()
        for copy in copies:
            copy.wait()

    @pl.when(even)
    def _():
        send(a_ref, b_ref)

    @pl.when(jnp.logical_not(even))
    def _():
        send(b_ref, a_ref)


def rims(c, ra_ref, rb_ref, lanes):
    even = lax.axis_index("rows") % 2 == 0
    ra = ra_ref[c, :, lanes].astype(jnp.float32)
    rb = rb_ref[c, :, lanes].astype(jnp.float32)
    return jnp.where(even, rb, ra), jnp.where(even, ra, rb)[0:8]


def col_edges_kernel(slide, ra_ref, rb_ref, a_ref, b_ref):
    even = lax.axis_index("cols") % 2 == 0
    lane = lanes_of((STRIP, 128))
    first = jnp.zeros((STRIP, 128), jnp.float32)
    last = jnp.zeros((STRIP, 128), jnp.float32)
    for c in range(3):
        sides = []
        for lanes in (slice(0, 128), slice(384, 512)):
            above, below = rims(c, ra_ref, rb_ref, lanes)
            sides.append(jnp.concatenate([above, slide[c, :, lanes].astype(jnp.float32), below], axis=0))
        for half in range(2):
            g = BEFORE * (2 * c + half)
            rows = slice(half * STRIP, half * STRIP + STRIP)
            lo = pltpu.roll(sides[0][rows], g, 1) if g else sides[0][rows]
            hi = pltpu.roll(sides[1][rows], (g + BEFORE) % 128, 1)
            first = jnp.where((lane >= g) & (lane < g + AFTER), lo, first)
            last = jnp.where((lane >= g) & (lane < g + BEFORE), hi, last)
    a_ref[...] = jnp.where(even, last, first).astype(jnp.bfloat16)
    b_ref[...] = jnp.where(even, first, last).astype(jnp.bfloat16)


def band_kernel(taps_ref, toep):
    def band(k, carry):
        base = pl.multiple_of(k * 128, 128)
        toep[pl.ds(base, 128), :] = jnp.zeros((128, BLOCK_LANES), jnp.bfloat16)
        p0 = taps_ref[k, 0:16, :]
        p1 = taps_ref[k, 16:32, :]
        p2 = taps_ref[k, 32:48, :]
        for m in range(BLOCK_LANES // 256):
            toep[pl.ds(base + 16 * m, 16), 256 * m : 256 * m + 128] = p0
            toep[pl.ds(base + 16 * m, 16), 256 * m + 128 : 256 * m + 256] = p1
            toep[pl.ds(base + 16 * m + 16, 16), 256 * m + 128 : 256 * m + 256] = p2
        return carry

    lax.fori_loop(0, TAPS1, band, 0)


def picks(first):
    lane = lax.broadcasted_iota(jnp.int32, (256, 128), 1)
    source = lax.broadcasted_iota(jnp.int32, (256, 128), 0)
    out = []
    for b, start in zip(range(BLOCKS), (0, 0, 128, 256, 256)):
        if b in first:
            hit = source + start == lane + (4 * BLOCK_COLS * b - BEFORE)
            out.append(jnp.where(hit, 1.0, 0.0).astype(jnp.bfloat16))
    return jnp.concatenate(out, axis=1)


def cut(rows):
    parts = []
    for blocks, start in (((0, 1), 0), ((2,), 128), ((3, 4), 256)):
        moved = jnp.dot(rows[:, start : start + 256], picks(blocks), preferred_element_type=jnp.float32)
        parts += [moved[:, 128 * i : 128 * i + 128] for i in range(len(blocks))]
    return parts


def window_kernel(slide, xb, lhs1):
    for c in range(3):
        for b, part in enumerate(cut(slide[c])):
            xb[b, c, RIM : RIM + 256, :] = part
    for b in range(BLOCKS):
        for c in range(3):
            for kh in range(6):
                k = 6 * c + kh
                lhs1[MID * b : MID * b + MID, 128 * k : 128 * k + 128] = xb[
                    b, c, pl.ds(RIM - BEFORE + kh + 4 * EDGE, MID, stride=4), :
                ].astype(jnp.bfloat16)


def patch_rows(ref, at, lhs1, slot):
    for c in range(3):
        for kh in range(6):
            k = 6 * c + kh
            lhs1[ROWS1 * slot : ROWS1 * slot + ROWS1, 128 * k : 128 * k + 128] = ref[
                at, c, pl.ds(RIM - BEFORE + kh, ROWS1, stride=4), :
            ].astype(jnp.bfloat16)


def inner_kernel(ra_ref, rb_ref, toep, xb_in, lhs1_in, xb, fmap, lhs1):
    outer = []
    for c in range(3):
        outer += rims(c, ra_ref, rb_ref, slice(None))
    parts = cut(jnp.concatenate(outer, axis=0).astype(jnp.bfloat16))
    for b in range(BLOCKS):
        for c in range(3):
            xb[b, c, 0:RIM, :] = parts[b][32 * c : 32 * c + RIM]
            xb[b, c, 280:288, :] = parts[b][32 * c + RIM : 32 * c + 32]
            xb[b, c, 288:328, :] = jnp.zeros((40, 128), jnp.float32)
    top, bottom = MID * BLOCKS, (MID + EDGE) * BLOCKS
    for c in range(3):
        for kh in range(6):
            lanes = slice(128 * (6 * c + kh), 128 * (6 * c + kh) + 128)
            low = []
            for b in range(BLOCKS):
                lhs1[top + EDGE * b : top + EDGE * b + EDGE, lanes] = xb[
                    b, c, pl.ds(RIM - BEFORE + kh, EDGE, stride=4), :
                ].astype(jnp.bfloat16)
                low.append(xb[b, c, pl.ds(RIM - BEFORE + kh + 4 * (EDGE + MID), 8, stride=4), :])
            low.append(jnp.zeros((8, 128), jnp.float32))
            lhs1[bottom : bottom + 48, lanes] = jnp.concatenate(low, axis=0).astype(jnp.bfloat16)
    for n in range(BLOCK_LANES // 256):
        acc = gelu(jnp.dot(lhs1[...], toep[:, 256 * n : 256 * n + 256], preferred_element_type=jnp.float32))
        for b in range(BLOCKS):
            for u in range(2):
                half = slice(128 * u, 128 * u + 128)
                fmap[b, 2 * n + u, 0:EDGE, :] = acc[top + EDGE * b : top + EDGE * b + EDGE, half]
                fmap[b, 2 * n + u, EDGE : EDGE + MID, :] = acc[MID * b : MID * b + MID, half]
                fmap[b, 2 * n + u, EDGE + MID : EDGE + MID + 8, :] = acc[bottom + 8 * b : bottom + 8 * b + 8, half]


def stem_kernel(
    ca_ref, cb_ref, xb_in, fmap_in, toep, w2, w3, wk_far, wv_far,
    xb, fmap, normed, wk, wv,
    lhs1, lhs2, smap, lhs3, third, sems,
    *, col_last, row_last,
):
    copies = [pltpu.make_async_copy(wk_far, wk, sems.at[0]), pltpu.make_async_copy(wv_far, wv, sems.at[1])]
    for copy in copies:
        copy.start()
    col = lax.axis_index("cols")
    row = lax.axis_index("rows")
    even_col = col % 2 == 0
    lane = lanes_of((STRIP, 128))
    ca = ca_ref[...].astype(jnp.float32)
    cb = cb_ref[...].astype(jnp.float32)
    left_all = jnp.where(even_col, cb, ca)
    right_all = jnp.where(even_col, ca, cb)
    at_right = 512 + BEFORE - 4 * BLOCK_COLS * (BLOCKS - 1)
    for c in range(3):
        for half in range(2):
            g = BEFORE * (2 * c + half)
            rows = slice(half * STRIP, half * STRIP + STRIP)
            left = pltpu.roll(left_all, 128 - g, 1) if g else left_all
            right = pltpu.roll(right_all, (at_right - g) % 128, 1)
            xb[0, c, rows, :] = jnp.where(lane < BEFORE, left, xb[0, c, rows, :])
            xb[BLOCKS - 1, c, rows, :] = jnp.where(
                (lane >= at_right) & (lane < at_right + AFTER), right, xb[BLOCKS - 1, c, rows, :]
            )
    patch_rows(xb, 0, lhs1, 0)
    patch_rows(xb, BLOCKS - 1, lhs1, 1)
    for slot, b, tiles in ((0, 0, (0, 1)), (1, BLOCKS - 1, (5,))):
        for n in tiles:
            acc = gelu(
                jnp.dot(
                    lhs1[ROWS1 * slot : ROWS1 * slot + ROWS1, :],
                    toep[:, 256 * n : 256 * n + 256],
                    preferred_element_type=jnp.float32,
                )
            )
            for u in range(2):
                fmap[b, 2 * n + u, 0:ROWS1, :] = acc[:, 128 * u : 128 * u + 128]

    @pl.when(row == 0)
    def _():
        for b in range(BLOCKS):
            fmap[b, :, 0:5, :] = jnp.zeros((BLOCK_LANES // 128, 5, 128), jnp.float32)

    @pl.when(row == row_last)
    def _():
        for b in range(BLOCKS):
            fmap[b, :, 69:70, :] = jnp.zeros((BLOCK_LANES // 128, 1, 128), jnp.float32)

    @pl.when(col == 0)
    def _():
        fmap[0, 0:2, 0:ROWS1, :] = jnp.zeros((2, ROWS1, 128), jnp.float32)
        fmap[0, 2, 0:ROWS1, 0:64] = jnp.zeros((ROWS1, 64), jnp.float32)

    @pl.when(col == col_last)
    def _():
        tile, side = divmod(133 - 4 * BLOCK_COLS, 2)
        fmap[4, tile, 0:ROWS1, 64 * side : 64 * side + 64] = jnp.zeros((ROWS1, 64), jnp.float32)

    for kh in range(6):
        for pair in range(COLS2 // 2):
            both = []
            for j in (2 * pair, 2 * pair + 1):
                b, t = divmod(j, 7)
                rows = pl.ds(kh, ROWS2, stride=4)
                tiles = [divmod(14 * b + 2 * t + u, 14) for u in range(3)]
                both.append([fmap[block, tile, rows, :] for block, tile in tiles])
            for u in range(3):
                lhs2[48 * pair : 48 * pair + 48, 384 * kh + 128 * u : 384 * kh + 128 * u + 128] = jnp.concatenate(
                    [both[0][u], both[1][u]], axis=0
                ).astype(jnp.bfloat16)
    for start, size in ((0, 288), (288, 288), (576, 240)):
        acc = gelu(jnp.dot(lhs2[start : start + size, :], w2[...], preferred_element_type=jnp.float32))
        for u in range(2):
            smap[u, start // ROWS2 : (start + size) // ROWS2] = acc[:, 128 * u : 128 * u + 128].reshape(
                size // ROWS2, ROWS2, 128
            )

    @pl.when(row == 0)
    def _():
        smap[:, :, 0:1, :] = jnp.zeros((2, COLS2, 1, 128), jnp.float32)

    @pl.when(col == 0)
    def _():
        smap[:, 0] = jnp.zeros((2, ROWS2, 128), jnp.float32)

    for kh in range(3):
        for kw in range(3):
            k = 3 * kh + kw
            for pair in range(8):
                for u in range(2):
                    lhs3[16 * pair : 16 * pair + 16, 256 * k + 128 * u : 256 * k + 128 * u + 128] = jnp.concatenate(
                        [
                            smap[u, 4 * pair + 2 * v + kw, pl.ds(kh, 8, stride=2), :]
                            for v in range(2)
                        ],
                        axis=0,
                    ).astype(jnp.bfloat16)

    for n in range(4):
        lanes = slice(256 * n, 256 * n + 256)
        third[:, lanes] = jnp.dot(lhs3[...], w3[:, lanes], preferred_element_type=jnp.float32)
    tokens = third[...]
    centred = tokens - jnp.mean(tokens, axis=-1, keepdims=True)
    var = jnp.mean(centred * centred, axis=-1, keepdims=True)
    normed[...] = (centred * lax.rsqrt(var + 1e-05)).astype(jnp.bfloat16)
    for copy in copies:
        copy.wait()


def project_kernel(mine, theirs, wk, wv, kv, tokens):
    half = mine.shape[0]
    tokens[0:half] = mine[...]
    tokens[half:] = theirs[...]
    for i, w in enumerate((wk, wv)):
        for n in range(4):
            rows = jnp.dot(tokens[...], w[:, 256 * n : 256 * n + 256], preferred_element_type=jnp.float32)
            kv[:, 1024 * i + 256 * n : 1024 * i + 256 * n + 256] = rows.astype(jnp.bfloat16)


def attend_kernel(q, kv, lead, lag, *, bit_of, chunk_of, keep):
    half = lead.shape[0]
    n = 2 * half
    quarter = 2 * (lax.axis_index("rows") % 2) + (bit_of() if keep else 1 - bit_of())
    rows = pl.ds(pl.multiple_of(quarter * n, n), n)
    upper = chunk_of() == 1

    def put(lanes, value):
        lead[:, lanes] = jnp.where(upper, value[:half], value[half:]).astype(lead.dtype)
        lag[:, lanes] = jnp.where(upper, value[half:], value[:half]).astype(lag.dtype)

    scale = 1.0 / math.sqrt(128)
    lane = lanes_of((n, 128))
    stat = jnp.zeros((n, 128), jnp.float32)
    for h in range(HEADS):
        lanes = slice(128 * h, 128 * h + 128)
        past = slice(1024 + 128 * h, 1024 + 128 * h + 128)
        scores = lax.dot_general(
            q[rows, lanes], kv[:, lanes], (((1,), (1,)), ((), ())), preferred_element_type=jnp.float32
        ) * scale
        peak = jnp.max(scores, axis=1, keepdims=True)
        w = jnp.exp(scores - peak)
        total = jnp.sum(w, axis=1, keepdims=True)
        o = jnp.dot(w.astype(jnp.bfloat16), kv[:, past], preferred_element_type=jnp.float32)
        put(lanes, o * (1.0 / total))
        stat = jnp.where(lane == h, peak + jnp.log(total), stat)
    put(slice(1024, 1152), stat if keep else pack_stat(stat).astype(jnp.float32))


def pack_stat(stat):
    lane = lanes_of(stat.shape)
    stat = jnp.where(lane < HEADS, stat, 0.0)
    high = stat.astype(jnp.bfloat16).astype(jnp.float32)
    rest = stat - high
    mid = rest.astype(jnp.bfloat16).astype(jnp.float32)
    low = rest - mid
    return (high + pltpu.roll(mid, HEADS, 1) + pltpu.roll(low, 2 * HEADS, 1)).astype(jnp.bfloat16)


def unpack_stat(stat):
    stat = stat.astype(jnp.float32)
    return stat + pltpu.roll(stat, 128 - HEADS, 1) + pltpu.roll(stat, 128 - 2 * HEADS, 1)


def merge_kernel(keep_ref, recv_ref, *outs, bit_of):
    n = keep_ref.shape[0]
    mine = keep_ref[:, 1024:1152]
    theirs = unpack_stat(recv_ref[:, 1024:1152])
    peak = jnp.maximum(mine, theirs)
    em = jnp.exp(mine - peak)
    total = em + jnp.exp(theirs - peak)
    share = em / total
    stat = peak + jnp.log(total)
    merged = []
    for h in range(HEADS):
        lanes = slice(128 * h, 128 * h + 128)
        a = keep_ref[:, lanes]
        b = recv_ref[:, lanes].astype(jnp.float32)
        merged.append(b + jnp.broadcast_to(share[:, h : h + 1], (n, 128)) * (a - b))
    if not callable(bit_of):
        for h in range(HEADS):
            outs[0][:, 128 * h : 128 * h + 128] = merged[h].astype(outs[0].dtype)
        if bit_of != "result":
            outs[0][:, 1024:1152] = pack_stat(stat) if bit_of == "send" else stat
        return
    upper = bit_of() == 1
    half = n // 2
    for h in range(HEADS):
        lanes = slice(128 * h, 128 * h + 128)
        outs[0][:, lanes] = jnp.where(upper, merged[h][half:], merged[h][:half])
        outs[1][:, lanes] = jnp.where(upper, merged[h][:half], merged[h][half:]).astype(jnp.bfloat16)
    outs[0][:, 1024:1152] = jnp.where(upper, stat[half:], stat[:half])
    outs[1][:, 1024:1152] = pack_stat(jnp.where(upper, stat[:half], stat[half:]))


def call(kernel, name, args, outs, scratch=(), aliases=None, flops=0, moved=0, limit=None, far=()):
    spec = pl.BlockSpec(memory_space=VMEM)
    far_spec = pl.BlockSpec(memory_space=pltpu.HBM)
    return pl.pallas_call(
        kernel,
        in_specs=[far_spec if i in far else spec for i in range(len(args))],
        out_specs=[spec] * len(outs),
        out_shape=tuple(outs),
        scratch_shapes=list(scratch),
        input_output_aliases=aliases or {},
        cost_estimate=pl.CostEstimate(flops=flops, bytes_accessed=moved, transcendentals=0),
        compiler_params=pltpu.CompilerParams(vmem_limit_bytes=limit),
        name=name,
    )(*[pltpu.with_memory_space_constraint(x, pltpu.HBM if i in far else VMEM) for i, x in enumerate(args)])


def merge(keep, recv, bit_of):
    n, width = keep.shape
    if bit_of == "result":
        outs = (jax.ShapeDtypeStruct((n, 1024), jnp.bfloat16),)
    elif not callable(bit_of):
        outs = (VMEM((n, width), jnp.bfloat16 if bit_of == "send" else jnp.float32),)
    else:
        outs = (VMEM((n // 2, width), jnp.float32), VMEM((n // 2, width), jnp.bfloat16))
    out = call(functools.partial(merge_kernel, bit_of=bit_of), "merge", (keep, recv), outs, limit=8 << 20)
    return out if callable(bit_of) else out[0]


def swap_pairs(size, odd):
    pairs = []
    for i in range(1 if odd else 0, size - 1, 2):
        pairs += [(i, i + 1), (i + 1, i)]
    return pairs


def bits_of(size):
    return size.bit_length() - 1


def plan(mesh):
    n_rows, n_cols = mesh.shape["rows"], mesh.shape["cols"]
    row_bits = [("rows", k) for k in range(1, bits_of(n_rows))]
    col_bits = [("cols", k) for k in range(bits_of(n_cols))]
    return row_bits + col_bits, col_bits[:1] + row_bits + col_bits[1:]


def solution(mesh):
    n_rows, n_cols = mesh.shape["rows"], mesh.shape["cols"]
    orders = plan(mesh)

    def partner(index, stage):
        col, row = divmod(index, n_rows)
        axis, k = orders[row & 1][stage]
        return col * n_rows + (row ^ (1 << k)) if axis == "rows" else (col ^ (1 << k)) * n_rows + row

    def exchange(value, stage):
        pairs = [(i, partner(i, stage)) for i in range(n_rows * n_cols)]
        return lax.ppermute(value, ("cols", "rows"), pairs)

    def bit_of(stage):
        def read():
            row = lax.axis_index("rows")
            (axis0, k0), (axis1, k1) = orders[0][stage], orders[1][stage]
            return jnp.where(
                row % 2 == 0, (lax.axis_index(axis0) >> k0) & 1, (lax.axis_index(axis1) >> k1) & 1
            )

        return read

    def order_queries(queries):
        latents, width = queries.shape
        share = latents // (n_rows * n_cols)
        names = [("cols", k) for k in reversed(range(bits_of(n_cols)))]
        names += [("rows", k) for k in reversed(range(bits_of(n_rows)))]
        split = queries.reshape([2] * len(names) + [share, width])
        at = names.index(("rows", 0))
        rest = names[:at] + names[at + 1 :]
        halves = []
        for core in range(2):
            part = lax.index_in_dim(split, core, at, keepdims=False)
            order = orders[core]
            axes = [rest.index(name) for name in order[:1] + order[2:3] + order[1:2] + order[3:]]
            halves.append(part.transpose(axes + [len(rest), len(rest) + 1]).reshape(latents // 2, width))
        return jnp.concatenate(halves, axis=0)

    def on_device(slide_pixels, stem_first, stem_second, stem_third, key_weight, value_weight, queries):
        bf16, f32 = jnp.bfloat16, jnp.float32
        rim = VMEM((3, RIM, 512), bf16)
        row_a, row_b = call(
            row_edges_kernel,
            "row_edges",
            (slide_pixels,),
            (rim, rim),
            scratch=[pltpu.SemaphoreType.DMA((2,))],
            limit=8 << 20,
            far=(0,),
        )
        row_a = lax.ppermute(row_a, "rows", swap_pairs(n_rows, False))
        row_b = lax.ppermute(row_b, "rows", swap_pairs(n_rows, True))
        strip = VMEM((STRIP, 128), bf16)
        col_a, col_b = call(
            col_edges_kernel, "col_edges", (slide_pixels, row_a, row_b), (strip, strip), limit=8 << 20
        )
        col_a = lax.ppermute(col_a, "cols", swap_pairs(n_cols, False))
        col_b = lax.ppermute(col_b, "cols", swap_pairs(n_cols, True))

        taps = stem_first.transpose(2, 0, 1, 3).reshape(TAPS1, 6, 64)
        taps = sum(
            jnp.pad(taps, ((0, 0), (top, 42 - top), (64 * side, 64 - 64 * side)))
            for top, side in ((0, 0), (4, 1), (24, 0), (28, 1))
        )
        (toep,) = call(
            band_kernel, "band", (taps,), (VMEM((TAPS1 * 128, BLOCK_LANES), bf16),), moved=4 << 20, limit=2 << 20
        )
        xb_shape = VMEM((BLOCKS, 3, 328, 128), f32)
        lhs1_shape = VMEM((ROWS_ALL, TAPS1 * 128), bf16)
        fmap_shape = VMEM((BLOCKS, BLOCK_LANES // 128, 104, 128), f32)
        xb, lhs1 = call(
            window_kernel, "windows", (slide_pixels,), (xb_shape, lhs1_shape), flops=1 << 28, moved=4 << 20, limit=8 << 20
        )
        xb, fmap, _ = call(
            inner_kernel,
            "inner",
            (row_a, row_b, toep, xb, lhs1),
            (xb_shape, fmap_shape, lhs1_shape),
            aliases={3: 0, 4: 2},
            flops=2 * ROWS_ALL * TAPS1 * 128 * BLOCK_LANES,
            moved=16 << 20,
            limit=8 << 20,
        )
        _, _, normed, key_near, value_near = call(
            functools.partial(stem_kernel, col_last=n_cols - 1, row_last=n_rows - 1),
            "stem",
            (
                col_a, col_b, xb, fmap, toep, stem_second.reshape(2304, 256), stem_third.reshape(2304, 1024),
                key_weight, value_weight,
            ),
            (xb_shape, fmap_shape, VMEM((128, 1024), bf16), VMEM((1024, 1024), bf16), VMEM((1024, 1024), bf16)),
            scratch=[
                pltpu.VMEM((2 * ROWS1, TAPS1 * 128), bf16),
                pltpu.VMEM((COLS2 * ROWS2, 2304), bf16),
                pltpu.VMEM((2, COLS2, ROWS2, 128), f32),
                pltpu.VMEM((128, 2304), bf16),
                pltpu.VMEM((128, 1024), f32),
                pltpu.SemaphoreType.DMA((2,)),
            ],
            aliases={2: 0, 3: 1},
            far=(7, 8),
            flops=3 << 30,
            limit=16 << 20,
        )
        normed_other = lax.ppermute(normed, "rows", swap_pairs(n_rows, False))
        (kv,) = call(
            project_kernel,
            "project",
            (normed, normed_other, key_near, value_near),
            (VMEM((256, 2048), bf16),),
            scratch=[pltpu.VMEM((256, 1024), bf16)],
            flops=1 << 30,
            limit=8 << 20,
        )
        ordered = order_queries(queries)
        eighth = queries.shape[0] // 8
        width = 1024 + STAT

        def attend(q, keep):
            shape = VMEM((eighth, width), f32 if keep else bf16)
            return call(
                functools.partial(attend_kernel, bit_of=bit_of(0), chunk_of=bit_of(2), keep=keep),
                "attend",
                (q, kv),
                (shape, shape),
                flops=1 << 30,
                limit=8 << 20,
            )

        sends = attend(ordered, False)
        ordered, lead, lag = lax.optimization_barrier((ordered, *sends))
        recvs = [exchange(lead, 0), exchange(lag, 0)]
        keeps = list(attend(ordered, True))
        for i in range(2):
            keeps[i], send = merge(keeps[i], recvs[i], bit_of(1))
            recvs[i] = exchange(send, 1)
        recv = exchange(merge(keeps[0], recvs[0], "send"), 2)
        keep = merge(keeps[1], recvs[1], "keep")
        for stage in range(3, len(orders[0])):
            keep, send = merge(keep, recv, bit_of(stage))
            recv = exchange(send, stage)
        return merge(keep, recv, "result")

    placed = (P(None, "rows", "cols"), P(), P(), P(), P(), P(), P())
    return jax.shard_map(
        on_device, mesh=mesh, in_specs=placed, out_specs=P(("cols", "rows"), None), check_vma=False
    )
```

```python
import functools
import math

import jax
import jax.numpy as jnp
from jax import lax
from jax.experimental import pallas as pl
from jax.experimental.pallas import tpu as pltpu
from jax.sharding import PartitionSpec as P

HEADS = 8
BEFORE, AFTER = 21, 5
TAPS1 = 18
BLOCK_COLS = 28
BLOCKS = 5
BLOCK_LANES = BLOCK_COLS * 64
HALF_LANES = BLOCK_LANES // 2
DEPTH1 = TAPS1 * 64
ROWS1 = 80
ROWS2 = 24
COLS2 = 34
STAT = 128
RIM = 24
EDGE, MID = 16, 48
MID_ALL, EDGE_ALL = MID * 5, EDGE * 5 + 48
STRIP = 144
VMEM = pltpu.MemorySpace.VMEM


def gelu(x):
    inner = x * (0.7978845608028654 + 0.035677408136300125 * (x * x))
    half = 0.5 * x
    return half + half * jnp.tanh(inner)


def lanes_of(shape):
    return lax.broadcasted_iota(jnp.int32, shape, len(shape) - 1)


def row_edges_kernel(slide_hbm, kernel_far, a_ref, b_ref, kernel, sems):
    extra = pltpu.make_async_copy(kernel_far, kernel, sems.at[2])
    extra.start()
    even = lax.axis_index("rows") % 2 == 0
    height = slide_hbm.shape[1]

    def send(first, second):
        copies = [
            pltpu.make_async_copy(slide_hbm.at[:, pl.ds(height - RIM, RIM), :], first, sems.at[0]),
            pltpu.make_async_copy(slide_hbm.at[:, pl.ds(0, RIM), :], second, sems.at[1]),
        ]
        for copy in copies:
            copy.start()
        for copy in copies:
            copy.wait()

    @pl.when(even)
    def _():
        send(a_ref, b_ref)

    @pl.when(jnp.logical_not(even))
    def _():
        send(b_ref, a_ref)

    extra.wait()


def rims(c, ra_ref, rb_ref, lanes):
    even = lax.axis_index("rows") % 2 == 0
    ra = ra_ref[c, :, lanes].astype(jnp.float32)
    rb = rb_ref[c, :, lanes].astype(jnp.float32)
    return jnp.where(even, rb, ra), jnp.where(even, ra, rb)[0:8]


def col_edges_kernel(slide, ra_ref, rb_ref, a_ref, b_ref):
    even = lax.axis_index("cols") % 2 == 0
    lane = lanes_of((STRIP, 128))
    first = jnp.zeros((STRIP, 128), jnp.float32)
    last = jnp.zeros((STRIP, 128), jnp.float32)
    for c in range(3):
        sides = []
        for lanes in (slice(0, 128), slice(384, 512)):
            above, below = rims(c, ra_ref, rb_ref, lanes)
            sides.append(jnp.concatenate([above, slide[c, :, lanes].astype(jnp.float32), below], axis=0))
        for half in range(2):
            g = BEFORE * (2 * c + half)
            rows = slice(half * STRIP, half * STRIP + STRIP)
            lo = pltpu.roll(sides[0][rows], g, 1) if g else sides[0][rows]
            hi = pltpu.roll(sides[1][rows], (g + BEFORE) % 128, 1)
            first = jnp.where((lane >= g) & (lane < g + AFTER), lo, first)
            last = jnp.where((lane >= g) & (lane < g + BEFORE), hi, last)
    a_ref[...] = jnp.where(even, last, first).astype(jnp.bfloat16)
    b_ref[...] = jnp.where(even, first, last).astype(jnp.bfloat16)


def band_kernel(kernel_ref, toep, taps):
    taps[...] = jnp.zeros(taps.shape, jnp.float32)
    for kh in range(6):
        for kw in range(6):
            rows = kernel_ref[kh, kw].astype(jnp.float32)
            for c in range(3):
                for top, side in ((0, 0), (4, 1), (24, 0), (28, 1)):
                    taps[6 * c + kh, top + kw : top + kw + 1, 64 * side : 64 * side + 64] = rows[c : c + 1]

    def band(k, carry):
        channel, kh = k // 6, k % 6
        base = pl.multiple_of((3 * channel + kh % 3) * 128 + (kh // 3) * 64, 64)
        toep[pl.ds(base, 64), :] = jnp.zeros((64, HALF_LANES), jnp.bfloat16)
        p0 = taps[k, 0:16, :].astype(jnp.bfloat16)
        p1 = taps[k, 16:32, :].astype(jnp.bfloat16)
        p2 = taps[k, 32:48, :].astype(jnp.bfloat16)
        for m in range(HALF_LANES // 128):
            lanes = slice(128 * m, 128 * m + 128)
            if m % 2 == 0:
                toep[pl.ds(base + 8 * m, 16), lanes] = p0
            else:
                toep[pl.ds(base + 8 * m - 8, 16), lanes] = p1
                toep[pl.ds(base + 8 * m + 8, 16), lanes] = p2
        return carry

    lax.fori_loop(0, TAPS1, band, 0)


def picks(blocks, start):
    lane = lax.broadcasted_iota(jnp.int32, (256, 128), 1)
    source = lax.broadcasted_iota(jnp.int32, (256, 128), 0) + (start + BEFORE)
    out = []
    for b in blocks:
        at = 4 * BLOCK_COLS * b
        for low, high in ((0, 56), (56, 0)):
            want = jnp.where(lane < 64, lane + (at + low), lane + (at + high - 64))
            out.append(jnp.where(source == want, 1.0, 0.0).astype(jnp.bfloat16))
    return jnp.concatenate(out, axis=1)


def cut(rows):
    parts = []
    for blocks, start in (((0, 1), 0), ((2,), 128), ((3, 4), 256)):
        moved = jnp.dot(rows[:, start : start + 256], picks(blocks, start), preferred_element_type=jnp.float32)
        parts += [
            (moved[:, 256 * i : 256 * i + 128], moved[:, 256 * i + 128 : 256 * i + 256]) for i in range(len(blocks))
        ]
    return parts


def patches(xb, b, half, c, pair, start, count):
    low = lanes_of((count, 128)) < 64
    first = xb[half, b, c, pl.ds(RIM - BEFORE + start + pair, count, stride=4), :]
    second = xb[1 - half, b, c, pl.ds(RIM - BEFORE + start + pair + 3, count, stride=4), :]
    return jnp.where(low, first, second)


def window_kernel(slide, toep, xb, fmap, lhs1):
    for c in range(3):
        for b, part in enumerate(cut(slide[c])):
            for order in range(2):
                xb[order, b, c, RIM : RIM + 256, :] = part[order]
    for half in range(2):
        for b in range(BLOCKS):
            row0 = MID_ALL * half + MID * b
            for k in range(9):
                lhs1[row0 : row0 + MID, 128 * k : 128 * k + 128] = patches(
                    xb, b, half, k // 3, k % 3, 4 * EDGE, MID
                ).astype(jnp.bfloat16)
    for start in range(0, HALF_LANES, 256):
        size = min(256, HALF_LANES - start)
        acc = gelu(jnp.dot(lhs1[...], toep[:, start : start + size], preferred_element_type=jnp.float32))
        for half in range(2):
            for b in range(BLOCKS):
                row0 = MID_ALL * half + MID * b
                for u in range(size // 128):
                    tile = (HALF_LANES * half + start) // 128 + u
                    fmap[b, tile, EDGE : EDGE + MID, :] = acc[row0 : row0 + MID, 128 * u : 128 * u + 128]


def inner_kernel(ra_ref, rb_ref, toep, xb_in, fmap_in, xb, fmap, lhs1, *, row_last):
    outer = []
    for c in range(3):
        outer += rims(c, ra_ref, rb_ref, slice(None))
    parts = cut(jnp.concatenate(outer, axis=0).astype(jnp.bfloat16))
    for b in range(BLOCKS):
        for c in range(3):
            for order in range(2):
                xb[order, b, c, 0:RIM, :] = parts[b][order][32 * c : 32 * c + RIM]
                xb[order, b, c, 280:288, :] = parts[b][order][32 * c + RIM : 32 * c + 32]
                xb[order, b, c, 288:328, :] = jnp.zeros((40, 128), jnp.float32)
    for half in range(2):
        top = EDGE_ALL * half
        bottom = top + EDGE * BLOCKS
        for k in range(9):
            lanes = slice(128 * k, 128 * k + 128)
            low = []
            for b in range(BLOCKS):
                lhs1[top + EDGE * b : top + EDGE * b + EDGE, lanes] = patches(
                    xb, b, half, k // 3, k % 3, 0, EDGE
                ).astype(jnp.bfloat16)
                low.append(patches(xb, b, half, k // 3, k % 3, 4 * (EDGE + MID), 8))
            low.append(jnp.zeros((8, 128), jnp.float32))
            lhs1[bottom : bottom + 48, lanes] = jnp.concatenate(low, axis=0).astype(jnp.bfloat16)
    for start in range(0, HALF_LANES, 256):
        size = min(256, HALF_LANES - start)
        acc = gelu(jnp.dot(lhs1[...], toep[:, start : start + size], preferred_element_type=jnp.float32))
        for half in range(2):
            top = EDGE_ALL * half
            bottom = top + EDGE * BLOCKS
            for b in range(BLOCKS):
                for u in range(size // 128):
                    tile = (HALF_LANES * half + start) // 128 + u
                    lanes = slice(128 * u, 128 * u + 128)
                    fmap[b, tile, 0:EDGE, :] = acc[top + EDGE * b : top + EDGE * b + EDGE, lanes]
                    fmap[b, tile, EDGE + MID : EDGE + MID + 8, :] = acc[bottom + 8 * b : bottom + 8 * b + 8, lanes]
    blank_rows(fmap, range(BLOCKS), row_last)


def blank_rows(fmap, blocks, row_last):
    row = lax.axis_index("rows")

    @pl.when(row == 0)
    def _():
        for b in blocks:
            fmap[b, :, 0:5, :] = jnp.zeros((BLOCK_LANES // 128, 5, 128), jnp.float32)

    @pl.when(row == row_last)
    def _():
        for b in blocks:
            fmap[b, :, 69:70, :] = jnp.zeros((BLOCK_LANES // 128, 1, 128), jnp.float32)


def second_map(cols, fmap, w2, lhs2, smap):
    for kh in range(6):
        rows = pl.ds(kh, ROWS2, stride=4)
        for i, col in enumerate(cols):
            for u in range(3):
                tiles = [divmod(2 * j + u, BLOCK_LANES // 128) for j in (col, col + 1)]
                lhs2[48 * i : 48 * i + 48, 384 * kh + 128 * u : 384 * kh + 128 * u + 128] = jnp.concatenate(
                    [fmap[block, tile, rows, :] for block, tile in tiles], axis=0
                ).astype(jnp.bfloat16)
    step = 5
    for start in range(0, len(cols), step):
        some = cols[start : start + step]
        acc = gelu(
            jnp.dot(lhs2[48 * start : 48 * (start + len(some)), :], w2[...], preferred_element_type=jnp.float32)
        )
        for i, col in enumerate(some):
            for u in range(2):
                smap[u, col : col + 2] = acc[48 * i : 48 * i + 48, 128 * u : 128 * u + 128].reshape(2, ROWS2, 128)


def middle_kernel(fmap, w2, smap, lhs2):
    second_map(range(2, COLS2 - 2, 2), fmap, w2, lhs2, smap)


def stem_kernel(
    ca_ref, cb_ref, xb_in, fmap_in, smap_in, toep, w2, w3, wk_far, wv_far,
    xb, fmap, smap, normed, wk, wv,
    lhs1, lhs2, lhs3, third, sems,
    *, col_last, row_last,
):
    copies = [pltpu.make_async_copy(wk_far, wk, sems.at[0]), pltpu.make_async_copy(wv_far, wv, sems.at[1])]
    for copy in copies:
        copy.start()
    col = lax.axis_index("cols")
    row = lax.axis_index("rows")
    even_col = col % 2 == 0
    lane = lanes_of((STRIP, 128))
    ca = ca_ref[...].astype(jnp.float32)
    cb = cb_ref[...].astype(jnp.float32)
    left_all = jnp.where(even_col, cb, ca)
    right_all = jnp.where(even_col, ca, cb)
    at_right = 512 + BEFORE - 4 * BLOCK_COLS * (BLOCKS - 1) - 56
    for c in range(3):
        for half in range(2):
            g = BEFORE * (2 * c + half)
            rows = slice(half * STRIP, half * STRIP + STRIP)
            for order in range(2):
                at = 64 * order
                left = pltpu.roll(left_all, (at - g) % 128, 1) if at != g else left_all
                here = (lane >= at) & (lane < at + BEFORE)
                xb[order, 0, c, rows, :] = jnp.where(here, left, xb[order, 0, c, rows, :])
                at = at_right + 64 * (1 - order)
                right = pltpu.roll(right_all, (at - g) % 128, 1)
                here = (lane >= at) & (lane < at + AFTER)
                xb[order, BLOCKS - 1, c, rows, :] = jnp.where(here, right, xb[order, BLOCKS - 1, c, rows, :])
    for k in range(9):
        for half, b in ((0, 0), (1, BLOCKS - 1)):
            lhs1[ROWS1 * half : ROWS1 * half + ROWS1, 128 * k : 128 * k + 128] = patches(
                xb, b, half, k // 3, k % 3, 0, ROWS1
            ).astype(jnp.bfloat16)
    for n in range(2):
        acc = gelu(jnp.dot(lhs1[...], toep[:, 256 * n : 256 * n + 256], preferred_element_type=jnp.float32))
        for u in range(2):
            fmap[0, 2 * n + u, 0:ROWS1, :] = acc[0:ROWS1, 128 * u : 128 * u + 128]
    fmap[BLOCKS - 1, 10, 0:ROWS1, :] = acc[ROWS1:, 128:256]

    blank_rows(fmap, (0, BLOCKS - 1), row_last)

    @pl.when(col == 0)
    def _():
        fmap[0, 0:2, 0:ROWS1, :] = jnp.zeros((2, ROWS1, 128), jnp.float32)
        fmap[0, 2, 0:ROWS1, 0:64] = jnp.zeros((ROWS1, 64), jnp.float32)

    @pl.when(col == col_last)
    def _():
        tile, side = divmod(133 - 4 * BLOCK_COLS, 2)
        fmap[4, tile, 0:ROWS1, 64 * side : 64 * side + 64] = jnp.zeros((ROWS1, 64), jnp.float32)

    second_map((0, COLS2 - 2), fmap, w2, lhs2, smap)

    @pl.when(row == 0)
    def _():
        smap[:, :, 0:1, :] = jnp.zeros((2, COLS2, 1, 128), jnp.float32)

    @pl.when(col == 0)
    def _():
        smap[:, 0] = jnp.zeros((2, ROWS2, 128), jnp.float32)

    for kh in range(3):
        for kw in range(3):
            k = 3 * kh + kw
            for pair in range(8):
                for u in range(2):
                    lhs3[16 * pair : 16 * pair + 16, 256 * k + 128 * u : 256 * k + 128 * u + 128] = jnp.concatenate(
                        [
                            smap[u, 4 * pair + 2 * v + kw, pl.ds(kh, 8, stride=2), :]
                            for v in range(2)
                        ],
                        axis=0,
                    ).astype(jnp.bfloat16)

    for n in range(4):
        lanes = slice(256 * n, 256 * n + 256)
        third[:, lanes] = jnp.dot(lhs3[...], w3[:, lanes], preferred_element_type=jnp.float32)
    tokens = third[...]
    centred = tokens - jnp.mean(tokens, axis=-1, keepdims=True)
    var = jnp.mean(centred * centred, axis=-1, keepdims=True)
    normed[...] = (centred * lax.rsqrt(var + 1e-05)).astype(jnp.bfloat16)
    for copy in copies:
        copy.wait()


def project_kernel(mine, theirs, wk, wv, kv, tokens):
    half = mine.shape[0]
    tokens[0:half] = mine[...]
    tokens[half:] = theirs[...]
    for i, w in enumerate((wk, wv)):
        for n in range(4):
            rows = jnp.dot(tokens[...], w[:, 256 * n : 256 * n + 256], preferred_element_type=jnp.float32)
            kv[:, 1024 * i + 256 * n : 1024 * i + 256 * n + 256] = rows.astype(jnp.bfloat16)


def attend_kernel(q, kv, lead, lag, *, bit_of, chunk_of, keep):
    half = lead.shape[0]
    n = 2 * half
    quarter = 2 * (lax.axis_index("rows") % 2) + (bit_of() if keep else 1 - bit_of())
    rows = pl.ds(pl.multiple_of(quarter * n, n), n)
    upper = chunk_of() == 1

    def put(lanes, value):
        lead[:, lanes] = jnp.where(upper, value[:half], value[half:]).astype(lead.dtype)
        lag[:, lanes] = jnp.where(upper, value[half:], value[:half]).astype(lag.dtype)

    scale = 1.0 / math.sqrt(128)
    lane = lanes_of((n, 128))
    stat = jnp.zeros((n, 128), jnp.float32)
    for h in range(HEADS):
        lanes = slice(128 * h, 128 * h + 128)
        past = slice(1024 + 128 * h, 1024 + 128 * h + 128)
        scores = lax.dot_general(
            q[rows, lanes], kv[:, lanes], (((1,), (1,)), ((), ())), preferred_element_type=jnp.float32
        ) * scale
        peak = jnp.max(scores, axis=1, keepdims=True)
        w = jnp.exp(scores - peak)
        total = jnp.sum(w, axis=1, keepdims=True)
        o = jnp.dot(w.astype(jnp.bfloat16), kv[:, past], preferred_element_type=jnp.float32)
        put(lanes, o * (1.0 / total))
        stat = jnp.where(lane == h, peak + jnp.log(total), stat)
    put(slice(1024, 1152), stat if keep else pack_stat(stat).astype(jnp.float32))


def pack_stat(stat):
    lane = lanes_of(stat.shape)
    stat = jnp.where(lane < HEADS, stat, 0.0)
    high = stat.astype(jnp.bfloat16).astype(jnp.float32)
    rest = stat - high
    mid = rest.astype(jnp.bfloat16).astype(jnp.float32)
    low = rest - mid
    return (high + pltpu.roll(mid, HEADS, 1) + pltpu.roll(low, 2 * HEADS, 1)).astype(jnp.bfloat16)


def unpack_stat(stat):
    stat = stat.astype(jnp.float32)
    return stat + pltpu.roll(stat, 128 - HEADS, 1) + pltpu.roll(stat, 128 - 2 * HEADS, 1)


def merge_kernel(keep_ref, recv_ref, *outs, bit_of):
    n = keep_ref.shape[0]
    mine = keep_ref[:, 1024:1152]
    theirs = unpack_stat(recv_ref[:, 1024:1152])
    peak = jnp.maximum(mine, theirs)
    em = jnp.exp(mine - peak)
    total = em + jnp.exp(theirs - peak)
    share = em / total
    stat = peak + jnp.log(total)
    merged = []
    for h in range(HEADS):
        lanes = slice(128 * h, 128 * h + 128)
        a = keep_ref[:, lanes]
        b = recv_ref[:, lanes].astype(jnp.float32)
        merged.append(b + jnp.broadcast_to(share[:, h : h + 1], (n, 128)) * (a - b))
    if not callable(bit_of):
        for h in range(HEADS):
            outs[0][:, 128 * h : 128 * h + 128] = merged[h].astype(outs[0].dtype)
        if bit_of != "result":
            outs[0][:, 1024:1152] = pack_stat(stat) if bit_of == "send" else stat
        return
    upper = bit_of() == 1
    half = n // 2
    for h in range(HEADS):
        lanes = slice(128 * h, 128 * h + 128)
        outs[0][:, lanes] = jnp.where(upper, merged[h][half:], merged[h][:half])
        outs[1][:, lanes] = jnp.where(upper, merged[h][:half], merged[h][half:]).astype(jnp.bfloat16)
    outs[0][:, 1024:1152] = jnp.where(upper, stat[half:], stat[:half])
    outs[1][:, 1024:1152] = pack_stat(jnp.where(upper, stat[:half], stat[half:]))


def call(kernel, name, args, outs, scratch=(), aliases=None, flops=0, moved=0, limit=None, far=()):
    spec = pl.BlockSpec(memory_space=VMEM)
    far_spec = pl.BlockSpec(memory_space=pltpu.HBM)
    return pl.pallas_call(
        kernel,
        in_specs=[far_spec if i in far else spec for i in range(len(args))],
        out_specs=[spec] * len(outs),
        out_shape=tuple(outs),
        scratch_shapes=list(scratch),
        input_output_aliases=aliases or {},
        cost_estimate=pl.CostEstimate(flops=flops, bytes_accessed=moved, transcendentals=0),
        compiler_params=pltpu.CompilerParams(vmem_limit_bytes=limit),
        name=name,
    )(*[pltpu.with_memory_space_constraint(x, pltpu.HBM if i in far else VMEM) for i, x in enumerate(args)])


def merge(keep, recv, bit_of):
    n, width = keep.shape
    if bit_of == "result":
        outs = (jax.ShapeDtypeStruct((n, 1024), jnp.bfloat16),)
    elif not callable(bit_of):
        outs = (VMEM((n, width), jnp.bfloat16 if bit_of == "send" else jnp.float32),)
    else:
        outs = (VMEM((n // 2, width), jnp.float32), VMEM((n // 2, width), jnp.bfloat16))
    out = call(functools.partial(merge_kernel, bit_of=bit_of), "merge", (keep, recv), outs, limit=8 << 20)
    return out if callable(bit_of) else out[0]


def swap_pairs(size, odd):
    pairs = []
    for i in range(1 if odd else 0, size - 1, 2):
        pairs += [(i, i + 1), (i + 1, i)]
    return pairs


def bits_of(size):
    return size.bit_length() - 1


def plan(mesh):
    n_rows, n_cols = mesh.shape["rows"], mesh.shape["cols"]
    row_bits = [("rows", k) for k in range(1, bits_of(n_rows))]
    col_bits = [("cols", k) for k in range(bits_of(n_cols))]
    return row_bits + col_bits, col_bits[:1] + row_bits + col_bits[1:]


def solution(mesh):
    n_rows, n_cols = mesh.shape["rows"], mesh.shape["cols"]
    orders = plan(mesh)

    def partner(index, stage):
        col, row = divmod(index, n_rows)
        axis, k = orders[row & 1][stage]
        return col * n_rows + (row ^ (1 << k)) if axis == "rows" else (col ^ (1 << k)) * n_rows + row

    def exchange(value, stage):
        pairs = [(i, partner(i, stage)) for i in range(n_rows * n_cols)]
        return lax.ppermute(value, ("cols", "rows"), pairs)

    def bit_of(stage):
        def read():
            row = lax.axis_index("rows")
            (axis0, k0), (axis1, k1) = orders[0][stage], orders[1][stage]
            return jnp.where(
                row % 2 == 0, (lax.axis_index(axis0) >> k0) & 1, (lax.axis_index(axis1) >> k1) & 1
            )

        return read

    def order_queries(queries):
        latents, width = queries.shape
        share = latents // (n_rows * n_cols)
        names = [("cols", k) for k in reversed(range(bits_of(n_cols)))]
        names += [("rows", k) for k in reversed(range(bits_of(n_rows)))]
        split = queries.reshape([2] * len(names) + [share, width])
        at = names.index(("rows", 0))
        rest = names[:at] + names[at + 1 :]
        halves = []
        for core in range(2):
            part = lax.index_in_dim(split, core, at, keepdims=False)
            order = orders[core]
            axes = [rest.index(name) for name in order[:1] + order[2:3] + order[1:2] + order[3:]]
            halves.append(part.transpose(axes + [len(rest), len(rest) + 1]).reshape(latents // 2, width))
        return jnp.concatenate(halves, axis=0)

    def on_device(slide_pixels, stem_first, stem_second, stem_third, key_weight, value_weight, queries):
        bf16, f32 = jnp.bfloat16, jnp.float32
        rim = VMEM((3, RIM, 512), bf16)
        row_a, row_b, first_near = call(
            row_edges_kernel,
            "row_edges",
            (slide_pixels, stem_first),
            (rim, rim, VMEM(stem_first.shape, bf16)),
            scratch=[pltpu.SemaphoreType.DMA((3,))],
            limit=8 << 20,
            far=(0, 1),
        )
        row_a = lax.ppermute(row_a, "rows", swap_pairs(n_rows, False))
        row_b = lax.ppermute(row_b, "rows", swap_pairs(n_rows, True))
        strip = VMEM((STRIP, 128), bf16)
        col_a, col_b = call(
            col_edges_kernel, "col_edges", (slide_pixels, row_a, row_b), (strip, strip), limit=8 << 20
        )
        col_a = lax.ppermute(col_a, "cols", swap_pairs(n_cols, False))
        col_b = lax.ppermute(col_b, "cols", swap_pairs(n_cols, True))

        (toep,) = call(
            band_kernel,
            "band",
            (first_near,),
            (VMEM((DEPTH1, HALF_LANES), bf16),),
            scratch=[pltpu.VMEM((TAPS1, 48, 128), f32)],
            moved=1 << 20,
            limit=4 << 20,
        )
        xb_shape = VMEM((2, BLOCKS, 3, 328, 128), f32)
        fmap_shape = VMEM((BLOCKS, BLOCK_LANES // 128, 104, 128), f32)
        xb, fmap = call(
            window_kernel,
            "windows",
            (slide_pixels, toep),
            (xb_shape, fmap_shape),
            scratch=[pltpu.VMEM((2 * MID_ALL, DEPTH1), bf16)],
            flops=2 * MID_ALL * DEPTH1 * BLOCK_LANES,
            moved=4 << 20,
            limit=8 << 20,
        )
        xb, fmap = call(
            functools.partial(inner_kernel, row_last=n_rows - 1),
            "inner",
            (row_a, row_b, toep, xb, fmap),
            (xb_shape, fmap_shape),
            scratch=[pltpu.VMEM((2 * EDGE_ALL, DEPTH1), bf16)],
            aliases={3: 0, 4: 1},
            flops=2 * EDGE_ALL * DEPTH1 * BLOCK_LANES,
            moved=16 << 20,
            limit=8 << 20,
        )
        smap_shape = VMEM((2, COLS2, ROWS2, 128), f32)
        w2 = stem_second.reshape(2304, 256)
        (smap,) = call(
            middle_kernel,
            "middle",
            (fmap, w2),
            (smap_shape,),
            scratch=[pltpu.VMEM(((COLS2 - 4) * ROWS2, 2304), bf16)],
            flops=2 * COLS2 * ROWS2 * 2304 * 256,
            moved=4 << 20,
            limit=8 << 20,
        )
        _, _, _, normed, key_near, value_near = call(
            functools.partial(stem_kernel, col_last=n_cols - 1, row_last=n_rows - 1),
            "stem",
            (
                col_a, col_b, xb, fmap, smap, toep, w2, stem_third.reshape(2304, 1024),
                key_weight, value_weight,
            ),
            (
                xb_shape, fmap_shape, smap_shape,
                VMEM((128, 1024), bf16), VMEM((1024, 1024), bf16), VMEM((1024, 1024), bf16),
            ),
            scratch=[
                pltpu.VMEM((2 * ROWS1, DEPTH1), bf16),
                pltpu.VMEM((4 * ROWS2, 2304), bf16),
                pltpu.VMEM((128, 2304), bf16),
                pltpu.VMEM((128, 1024), f32),
                pltpu.SemaphoreType.DMA((2,)),
            ],
            aliases={2: 0, 3: 1, 4: 2},
            far=(8, 9),
            flops=2 << 30,
            limit=8 << 20,
        )
        normed_other = lax.ppermute(normed, "rows", swap_pairs(n_rows, False))
        (kv,) = call(
            project_kernel,
            "project",
            (normed, normed_other, key_near, value_near),
            (VMEM((256, 2048), bf16),),
            scratch=[pltpu.VMEM((256, 1024), bf16)],
            flops=1 << 30,
            limit=8 << 20,
        )
        ordered = order_queries(queries)
        eighth = queries.shape[0] // 8
        width = 1024 + STAT

        def attend(q, keep):
            shape = VMEM((eighth, width), f32 if keep else bf16)
            return call(
                functools.partial(attend_kernel, bit_of=bit_of(0), chunk_of=bit_of(2), keep=keep),
                "attend",
                (q, kv),
                (shape, shape),
                flops=1 << 30,
                limit=8 << 20,
            )

        sends = attend(ordered, False)
        ordered, lead, lag = lax.optimization_barrier((ordered, *sends))
        recvs = [exchange(lead, 0), exchange(lag, 0)]
        keeps = list(attend(ordered, True))
        for i in range(2):
            keeps[i], send = merge(keeps[i], recvs[i], bit_of(1))
            recvs[i] = exchange(send, 1)
        recv = exchange(merge(keeps[0], recvs[0], "send"), 2)
        keep = merge(keeps[1], recvs[1], "keep")
        for stage in range(3, len(orders[0])):
            keep, send = merge(keep, recv, bit_of(stage))
            recv = exchange(send, stage)
        return merge(keep, recv, "result")

    placed = (P(None, "rows", "cols"), P(), P(), P(), P(), P(), P())
    return jax.shard_map(
        on_device, mesh=mesh, in_specs=placed, out_specs=P(("cols", "rows"), None), check_vma=False
    )
```

```python
import functools
import math

import jax
import jax.numpy as jnp
from jax import lax
from jax.experimental import pallas as pl
from jax.experimental.pallas import tpu as pltpu
from jax.sharding import PartitionSpec as P

HEADS = 8
BEFORE, AFTER = 21, 5
TAPS1 = 18
BLOCK_COLS = 28
BLOCKS = 5
BLOCK_LANES = BLOCK_COLS * 64
HALF_LANES = BLOCK_LANES // 2
DEPTH1 = TAPS1 * 64
ROWS1 = 80
ROWS2 = 24
COLS2 = 34
STAT = 128
RIM = 24
EDGE, MID = 16, 48
MID_ALL, EDGE_ALL = MID * 5, EDGE * 5 + 48
STRIP = 144
VMEM = pltpu.MemorySpace.VMEM


def gelu(x):
    inner = x * (0.7978845608028654 + 0.035677408136300125 * (x * x))
    half = 0.5 * x
    return half + half * jnp.tanh(inner)


def lanes_of(shape):
    return lax.broadcasted_iota(jnp.int32, shape, len(shape) - 1)


def row_edges_kernel(slide_hbm, kernel_far, a_ref, b_ref, kernel, sems):
    extra = pltpu.make_async_copy(kernel_far, kernel, sems.at[2])
    extra.start()
    even = lax.axis_index("rows") % 2 == 0
    height = slide_hbm.shape[1]

    def send(first, second):
        copies = [
            pltpu.make_async_copy(slide_hbm.at[:, pl.ds(height - RIM, RIM), :], first, sems.at[0]),
            pltpu.make_async_copy(slide_hbm.at[:, pl.ds(0, RIM), :], second, sems.at[1]),
        ]
        for copy in copies:
            copy.start()
        for copy in copies:
            copy.wait()

    @pl.when(even)
    def _():
        send(a_ref, b_ref)

    @pl.when(jnp.logical_not(even))
    def _():
        send(b_ref, a_ref)

    extra.wait()


def rims(c, ra_ref, rb_ref, lanes):
    even = lax.axis_index("rows") % 2 == 0
    ra = ra_ref[c, :, lanes].astype(jnp.float32)
    rb = rb_ref[c, :, lanes].astype(jnp.float32)
    return jnp.where(even, rb, ra), jnp.where(even, ra, rb)[0:8]


def col_edges_kernel(slide, ra_ref, rb_ref, a_ref, b_ref):
    even = lax.axis_index("cols") % 2 == 0
    lane = lanes_of((STRIP, 128))
    first = jnp.zeros((STRIP, 128), jnp.float32)
    last = jnp.zeros((STRIP, 128), jnp.float32)
    for c in range(3):
        sides = []
        for lanes in (slice(0, 128), slice(384, 512)):
            above, below = rims(c, ra_ref, rb_ref, lanes)
            sides.append(jnp.concatenate([above, slide[c, :, lanes].astype(jnp.float32), below], axis=0))
        for half in range(2):
            g = BEFORE * (2 * c + half)
            rows = slice(half * STRIP, half * STRIP + STRIP)
            lo = pltpu.roll(sides[0][rows], g, 1) if g else sides[0][rows]
            hi = pltpu.roll(sides[1][rows], (g + BEFORE) % 128, 1)
            first = jnp.where((lane >= g) & (lane < g + AFTER), lo, first)
            last = jnp.where((lane >= g) & (lane < g + BEFORE), hi, last)
    a_ref[...] = jnp.where(even, last, first).astype(jnp.bfloat16)
    b_ref[...] = jnp.where(even, first, last).astype(jnp.bfloat16)


def band_kernel(kernel_ref, toep, taps):
    taps[...] = jnp.zeros(taps.shape, jnp.float32)
    for kh in range(6):
        for kw in range(6):
            rows = kernel_ref[kh, kw].astype(jnp.float32)
            for c in range(3):
                for top, side in ((0, 0), (4, 1), (24, 0), (28, 1)):
                    taps[6 * c + kh, top + kw : top + kw + 1, 64 * side : 64 * side + 64] = rows[c : c + 1]

    def band(k, carry):
        channel, kh = k // 6, k % 6
        base = pl.multiple_of((3 * channel + kh % 3) * 128 + (kh // 3) * 64, 64)
        toep[pl.ds(base, 64), :] = jnp.zeros((64, HALF_LANES), jnp.bfloat16)
        p0 = taps[k, 0:16, :].astype(jnp.bfloat16)
        p1 = taps[k, 16:32, :].astype(jnp.bfloat16)
        p2 = taps[k, 32:48, :].astype(jnp.bfloat16)
        for m in range(HALF_LANES // 128):
            lanes = slice(128 * m, 128 * m + 128)
            if m % 2 == 0:
                toep[pl.ds(base + 8 * m, 16), lanes] = p0
            else:
                toep[pl.ds(base + 8 * m - 8, 16), lanes] = p1
                toep[pl.ds(base + 8 * m + 8, 16), lanes] = p2
        return carry

    lax.fori_loop(0, TAPS1, band, 0)


def picks(blocks, start):
    lane = lax.broadcasted_iota(jnp.int32, (256, 128), 1)
    source = lax.broadcasted_iota(jnp.int32, (256, 128), 0) + (start + BEFORE)
    out = []
    for b in blocks:
        at = 4 * BLOCK_COLS * b
        for low, high in ((0, 56), (56, 0)):
            want = jnp.where(lane < 64, lane + (at + low), lane + (at + high - 64))
            out.append(jnp.where(source == want, 1.0, 0.0).astype(jnp.bfloat16))
    return jnp.concatenate(out, axis=1)


def cut(rows):
    parts = []
    for blocks, start in (((0, 1), 0), ((2,), 128), ((3, 4), 256)):
        moved = jnp.dot(rows[:, start : start + 256], picks(blocks, start), preferred_element_type=jnp.float32)
        parts += [
            (moved[:, 256 * i : 256 * i + 128], moved[:, 256 * i + 128 : 256 * i + 256]) for i in range(len(blocks))
        ]
    return parts


def patches(xb, b, half, c, pair, start, count):
    low = lanes_of((count, 128)) < 64
    first = xb[half, b, c, pl.ds(RIM - BEFORE + start + pair, count, stride=4), :]
    second = xb[1 - half, b, c, pl.ds(RIM - BEFORE + start + pair + 3, count, stride=4), :]
    return jnp.where(low, first, second)


def window_kernel(slide, toep, far, xb, fmap, near, lhs1, sem):
    copy = pltpu.make_async_copy(far, near, sem)
    copy.start()
    for c in range(3):
        for b, part in enumerate(cut(slide[c])):
            for order in range(2):
                xb[order, b, c, RIM : RIM + 256, :] = part[order]
    for half in range(2):
        for b in range(BLOCKS):
            row0 = MID_ALL * half + MID * b
            for k in range(9):
                lhs1[row0 : row0 + MID, 128 * k : 128 * k + 128] = patches(
                    xb, b, half, k // 3, k % 3, 4 * EDGE, MID
                ).astype(jnp.bfloat16)
    for start in range(0, HALF_LANES, 256):
        size = min(256, HALF_LANES - start)
        acc = gelu(jnp.dot(lhs1[...], toep[:, start : start + size], preferred_element_type=jnp.float32))
        for half in range(2):
            for b in range(BLOCKS):
                row0 = MID_ALL * half + MID * b
                for u in range(size // 128):
                    tile = (HALF_LANES * half + start) // 128 + u
                    fmap[b, tile, EDGE : EDGE + MID, :] = acc[row0 : row0 + MID, 128 * u : 128 * u + 128]
    copy.wait()


def inner_kernel(ra_ref, rb_ref, toep, xb_in, fmap_in, xb, fmap, lhs1, *, row_last):
    outer = []
    for c in range(3):
        outer += rims(c, ra_ref, rb_ref, slice(None))
    parts = cut(jnp.concatenate(outer, axis=0).astype(jnp.bfloat16))
    for b in range(BLOCKS):
        for c in range(3):
            for order in range(2):
                xb[order, b, c, 0:RIM, :] = parts[b][order][32 * c : 32 * c + RIM]
                xb[order, b, c, 280:288, :] = parts[b][order][32 * c + RIM : 32 * c + 32]
                xb[order, b, c, 288:328, :] = jnp.zeros((40, 128), jnp.float32)
    for half in range(2):
        top = EDGE_ALL * half
        bottom = top + EDGE * BLOCKS
        for k in range(9):
            lanes = slice(128 * k, 128 * k + 128)
            low = []
            for b in range(BLOCKS):
                lhs1[top + EDGE * b : top + EDGE * b + EDGE, lanes] = patches(
                    xb, b, half, k // 3, k % 3, 0, EDGE
                ).astype(jnp.bfloat16)
                low.append(patches(xb, b, half, k // 3, k % 3, 4 * (EDGE + MID), 8))
            low.append(jnp.zeros((8, 128), jnp.float32))
            lhs1[bottom : bottom + 48, lanes] = jnp.concatenate(low, axis=0).astype(jnp.bfloat16)
    for start in range(0, HALF_LANES, 256):
        size = min(256, HALF_LANES - start)
        acc = gelu(jnp.dot(lhs1[...], toep[:, start : start + size], preferred_element_type=jnp.float32))
        for half in range(2):
            top = EDGE_ALL * half
            bottom = top + EDGE * BLOCKS
            for b in range(BLOCKS):
                for u in range(size // 128):
                    tile = (HALF_LANES * half + start) // 128 + u
                    lanes = slice(128 * u, 128 * u + 128)
                    fmap[b, tile, 0:EDGE, :] = acc[top + EDGE * b : top + EDGE * b + EDGE, lanes]
                    fmap[b, tile, EDGE + MID : EDGE + MID + 8, :] = acc[bottom + 8 * b : bottom + 8 * b + 8, lanes]
    blank_rows(fmap, range(BLOCKS), row_last)


def blank_rows(fmap, blocks, row_last):
    row = lax.axis_index("rows")

    @pl.when(row == 0)
    def _():
        for b in blocks:
            fmap[b, :, 0:5, :] = jnp.zeros((BLOCK_LANES // 128, 5, 128), jnp.float32)

    @pl.when(row == row_last)
    def _():
        for b in blocks:
            fmap[b, :, 69:70, :] = jnp.zeros((BLOCK_LANES // 128, 1, 128), jnp.float32)


def second_map(cols, fmap, w2, lhs2, smap):
    for kh in range(6):
        rows = pl.ds(kh, ROWS2, stride=4)
        for i, col in enumerate(cols):
            for u in range(3):
                tiles = [divmod(2 * j + u, BLOCK_LANES // 128) for j in (col, col + 1)]
                lhs2[48 * i : 48 * i + 48, 384 * kh + 128 * u : 384 * kh + 128 * u + 128] = jnp.concatenate(
                    [fmap[block, tile, rows, :] for block, tile in tiles], axis=0
                ).astype(jnp.bfloat16)
    step = 5
    for start in range(0, len(cols), step):
        some = cols[start : start + step]
        acc = gelu(
            jnp.dot(lhs2[48 * start : 48 * (start + len(some)), :], w2[...], preferred_element_type=jnp.float32)
        )
        for i, col in enumerate(some):
            for u in range(2):
                smap[u, col : col + 2] = acc[48 * i : 48 * i + 48, 128 * u : 128 * u + 128].reshape(2, ROWS2, 128)


def middle_kernel(fmap, w2, smap, lhs2):
    second_map(range(2, COLS2 - 2, 2), fmap, w2, lhs2, smap)


def stem_kernel(
    ca_ref, cb_ref, xb_in, fmap_in, smap_in, toep, w2, w3, far,
    xb, fmap, smap, normed, near,
    lhs1, lhs2, lhs3, third, sem,
    *, col_last, row_last,
):
    copy = pltpu.make_async_copy(far, near, sem)
    copy.start()
    col = lax.axis_index("cols")
    row = lax.axis_index("rows")
    even_col = col % 2 == 0
    lane = lanes_of((STRIP, 128))
    ca = ca_ref[...].astype(jnp.float32)
    cb = cb_ref[...].astype(jnp.float32)
    left_all = jnp.where(even_col, cb, ca)
    right_all = jnp.where(even_col, ca, cb)
    at_right = 512 + BEFORE - 4 * BLOCK_COLS * (BLOCKS - 1) - 56
    for c in range(3):
        for half in range(2):
            g = BEFORE * (2 * c + half)
            rows = slice(half * STRIP, half * STRIP + STRIP)
            for order in range(2):
                at = 64 * order
                left = pltpu.roll(left_all, (at - g) % 128, 1) if at != g else left_all
                here = (lane >= at) & (lane < at + BEFORE)
                xb[order, 0, c, rows, :] = jnp.where(here, left, xb[order, 0, c, rows, :])
                at = at_right + 64 * (1 - order)
                right = pltpu.roll(right_all, (at - g) % 128, 1)
                here = (lane >= at) & (lane < at + AFTER)
                xb[order, BLOCKS - 1, c, rows, :] = jnp.where(here, right, xb[order, BLOCKS - 1, c, rows, :])
    for k in range(9):
        for half, b in ((0, 0), (1, BLOCKS - 1)):
            lhs1[ROWS1 * half : ROWS1 * half + ROWS1, 128 * k : 128 * k + 128] = patches(
                xb, b, half, k // 3, k % 3, 0, ROWS1
            ).astype(jnp.bfloat16)
    for n in range(2):
        acc = gelu(jnp.dot(lhs1[...], toep[:, 256 * n : 256 * n + 256], preferred_element_type=jnp.float32))
        for u in range(2):
            fmap[0, 2 * n + u, 0:ROWS1, :] = acc[0:ROWS1, 128 * u : 128 * u + 128]
    fmap[BLOCKS - 1, 10, 0:ROWS1, :] = acc[ROWS1:, 128:256]

    blank_rows(fmap, (0, BLOCKS - 1), row_last)

    @pl.when(col == 0)
    def _():
        fmap[0, 0:2, 0:ROWS1, :] = jnp.zeros((2, ROWS1, 128), jnp.float32)
        fmap[0, 2, 0:ROWS1, 0:64] = jnp.zeros((ROWS1, 64), jnp.float32)

    @pl.when(col == col_last)
    def _():
        tile, side = divmod(133 - 4 * BLOCK_COLS, 2)
        fmap[4, tile, 0:ROWS1, 64 * side : 64 * side + 64] = jnp.zeros((ROWS1, 64), jnp.float32)

    second_map((0, COLS2 - 2), fmap, w2, lhs2, smap)

    @pl.when(row == 0)
    def _():
        smap[:, :, 0:1, :] = jnp.zeros((2, COLS2, 1, 128), jnp.float32)

    @pl.when(col == 0)
    def _():
        smap[:, 0] = jnp.zeros((2, ROWS2, 128), jnp.float32)

    for kh in range(3):
        for kw in range(3):
            k = 3 * kh + kw
            for pair in range(8):
                for u in range(2):
                    lhs3[16 * pair : 16 * pair + 16, 256 * k + 128 * u : 256 * k + 128 * u + 128] = jnp.concatenate(
                        [
                            smap[u, 4 * pair + 2 * v + kw, pl.ds(kh, 8, stride=2), :]
                            for v in range(2)
                        ],
                        axis=0,
                    ).astype(jnp.bfloat16)

    for n in range(4):
        lanes = slice(256 * n, 256 * n + 256)
        third[:, lanes] = jnp.dot(lhs3[...], w3[:, lanes], preferred_element_type=jnp.float32)
    tokens = third[...]
    centred = tokens - jnp.mean(tokens, axis=-1, keepdims=True)
    var = jnp.mean(centred * centred, axis=-1, keepdims=True)
    normed[...] = (centred * lax.rsqrt(var + 1e-05)).astype(jnp.bfloat16)
    copy.wait()


def project_kernel(tokens, wk, wv, kv):
    for i, w in enumerate((wk, wv)):
        for n in range(4):
            rows = jnp.dot(tokens[...], w[:, 256 * n : 256 * n + 256], preferred_element_type=jnp.float32)
            kv[:, 1024 * i + 256 * n : 1024 * i + 256 * n + 256] = rows.astype(jnp.bfloat16)


def attend_kernel(q, mine, theirs, lead, lag, *, bit_of, chunk_of, keep):
    half = lead.shape[0]
    n = 2 * half
    quarter = 2 * (lax.axis_index("rows") % 2) + (bit_of() if keep else 1 - bit_of())
    rows = pl.ds(pl.multiple_of(quarter * n, n), n)
    upper = chunk_of() == 1

    def put(lanes, value):
        lead[:, lanes] = jnp.where(upper, value[:half], value[half:]).astype(lead.dtype)
        lag[:, lanes] = jnp.where(upper, value[half:], value[:half]).astype(lag.dtype)

    scale = 1.0 / math.sqrt(128)
    lane = lanes_of((n, 128))
    stat = jnp.zeros((n, 128), jnp.float32)
    for h in range(HEADS):
        lanes = slice(128 * h, 128 * h + 128)
        past = slice(1024 + 128 * h, 1024 + 128 * h + 128)
        keys = jnp.concatenate([mine[:, lanes], theirs[:, lanes]], axis=0)
        values = jnp.concatenate([mine[:, past], theirs[:, past]], axis=0)
        scores = lax.dot_general(
            q[rows, lanes], keys, (((1,), (1,)), ((), ())), preferred_element_type=jnp.float32
        ) * scale
        peak = jnp.max(scores, axis=1, keepdims=True)
        w = jnp.exp(scores - peak)
        total = jnp.sum(w, axis=1, keepdims=True)
        o = jnp.dot(w.astype(jnp.bfloat16), values, preferred_element_type=jnp.float32)
        put(lanes, o * (1.0 / total))
        stat = jnp.where(lane == h, peak + jnp.log(total), stat)
    put(slice(1024, 1152), stat if keep else pack_stat(stat).astype(jnp.float32))


def pack_stat(stat):
    lane = lanes_of(stat.shape)
    stat = jnp.where(lane < HEADS, stat, 0.0)
    high = stat.astype(jnp.bfloat16).astype(jnp.float32)
    rest = stat - high
    mid = rest.astype(jnp.bfloat16).astype(jnp.float32)
    low = rest - mid
    return (high + pltpu.roll(mid, HEADS, 1) + pltpu.roll(low, 2 * HEADS, 1)).astype(jnp.bfloat16)


def unpack_stat(stat):
    stat = stat.astype(jnp.float32)
    return stat + pltpu.roll(stat, 128 - HEADS, 1) + pltpu.roll(stat, 128 - 2 * HEADS, 1)


def merge_kernel(keep_ref, recv_ref, *outs, bit_of):
    n = keep_ref.shape[0]
    mine = keep_ref[:, 1024:1152]
    theirs = unpack_stat(recv_ref[:, 1024:1152])
    peak = jnp.maximum(mine, theirs)
    em = jnp.exp(mine - peak)
    total = em + jnp.exp(theirs - peak)
    share = em / total
    stat = peak + jnp.log(total)
    merged = []
    for h in range(HEADS):
        lanes = slice(128 * h, 128 * h + 128)
        a = keep_ref[:, lanes]
        b = recv_ref[:, lanes].astype(jnp.float32)
        merged.append(b + jnp.broadcast_to(share[:, h : h + 1], (n, 128)) * (a - b))
    if not callable(bit_of):
        for h in range(HEADS):
            outs[0][:, 128 * h : 128 * h + 128] = merged[h].astype(outs[0].dtype)
        if bit_of != "result":
            outs[0][:, 1024:1152] = pack_stat(stat) if bit_of == "send" else stat
        return
    upper = bit_of() == 1
    half = n // 2
    for h in range(HEADS):
        lanes = slice(128 * h, 128 * h + 128)
        outs[0][:, lanes] = jnp.where(upper, merged[h][half:], merged[h][:half])
        outs[1][:, lanes] = jnp.where(upper, merged[h][:half], merged[h][half:]).astype(jnp.bfloat16)
    outs[0][:, 1024:1152] = jnp.where(upper, stat[half:], stat[:half])
    outs[1][:, 1024:1152] = pack_stat(jnp.where(upper, stat[:half], stat[half:]))


def call(kernel, name, args, outs, scratch=(), aliases=None, flops=0, moved=0, limit=None, far=()):
    spec = pl.BlockSpec(memory_space=VMEM)
    far_spec = pl.BlockSpec(memory_space=pltpu.HBM)
    return pl.pallas_call(
        kernel,
        in_specs=[far_spec if i in far else spec for i in range(len(args))],
        out_specs=[spec] * len(outs),
        out_shape=tuple(outs),
        scratch_shapes=list(scratch),
        input_output_aliases=aliases or {},
        cost_estimate=pl.CostEstimate(flops=flops, bytes_accessed=moved, transcendentals=0),
        compiler_params=pltpu.CompilerParams(vmem_limit_bytes=limit),
        name=name,
    )(*[pltpu.with_memory_space_constraint(x, pltpu.HBM if i in far else VMEM) for i, x in enumerate(args)])


def merge(keep, recv, bit_of):
    n, width = keep.shape
    if bit_of == "result":
        outs = (jax.ShapeDtypeStruct((n, 1024), jnp.bfloat16),)
    elif not callable(bit_of):
        outs = (VMEM((n, width), jnp.bfloat16 if bit_of == "send" else jnp.float32),)
    else:
        outs = (VMEM((n // 2, width), jnp.float32), VMEM((n // 2, width), jnp.bfloat16))
    out = call(functools.partial(merge_kernel, bit_of=bit_of), "merge", (keep, recv), outs, limit=8 << 20)
    return out if callable(bit_of) else out[0]


def swap_pairs(size, odd):
    pairs = []
    for i in range(1 if odd else 0, size - 1, 2):
        pairs += [(i, i + 1), (i + 1, i)]
    return pairs


def bits_of(size):
    return size.bit_length() - 1


def plan(mesh):
    n_rows, n_cols = mesh.shape["rows"], mesh.shape["cols"]
    row_bits = [("rows", k) for k in range(1, bits_of(n_rows))]
    col_bits = [("cols", k) for k in range(bits_of(n_cols))]
    return row_bits + col_bits, col_bits[:1] + row_bits + col_bits[1:]


def solution(mesh):
    n_rows, n_cols = mesh.shape["rows"], mesh.shape["cols"]
    orders = plan(mesh)

    def partner(index, stage):
        col, row = divmod(index, n_rows)
        axis, k = orders[row & 1][stage]
        return col * n_rows + (row ^ (1 << k)) if axis == "rows" else (col ^ (1 << k)) * n_rows + row

    def exchange(value, stage):
        pairs = [(i, partner(i, stage)) for i in range(n_rows * n_cols)]
        return lax.ppermute(value, ("cols", "rows"), pairs)

    def bit_of(stage):
        def read():
            row = lax.axis_index("rows")
            (axis0, k0), (axis1, k1) = orders[0][stage], orders[1][stage]
            return jnp.where(
                row % 2 == 0, (lax.axis_index(axis0) >> k0) & 1, (lax.axis_index(axis1) >> k1) & 1
            )

        return read

    def order_queries(queries):
        latents, width = queries.shape
        share = latents // (n_rows * n_cols)
        names = [("cols", k) for k in reversed(range(bits_of(n_cols)))]
        names += [("rows", k) for k in reversed(range(bits_of(n_rows)))]
        split = queries.reshape([2] * len(names) + [share, width])
        at = names.index(("rows", 0))
        rest = names[:at] + names[at + 1 :]
        halves = []
        for core in range(2):
            part = lax.index_in_dim(split, core, at, keepdims=False)
            order = orders[core]
            axes = [rest.index(name) for name in order[:1] + order[2:3] + order[1:2] + order[3:]]
            halves.append(part.transpose(axes + [len(rest), len(rest) + 1]).reshape(latents // 2, width))
        return jnp.concatenate(halves, axis=0)

    def on_device(slide_pixels, stem_first, stem_second, stem_third, key_weight, value_weight, queries):
        bf16, f32 = jnp.bfloat16, jnp.float32
        rim = VMEM((3, RIM, 512), bf16)
        row_a, row_b, first_near = call(
            row_edges_kernel,
            "row_edges",
            (slide_pixels, stem_first),
            (rim, rim, VMEM(stem_first.shape, bf16)),
            scratch=[pltpu.SemaphoreType.DMA((3,))],
            limit=8 << 20,
            far=(0, 1),
        )
        row_a = lax.ppermute(row_a, "rows", swap_pairs(n_rows, False))
        row_b = lax.ppermute(row_b, "rows", swap_pairs(n_rows, True))
        strip = VMEM((STRIP, 128), bf16)
        col_a, col_b = call(
            col_edges_kernel, "col_edges", (slide_pixels, row_a, row_b), (strip, strip), limit=8 << 20
        )
        col_a = lax.ppermute(col_a, "cols", swap_pairs(n_cols, False))
        col_b = lax.ppermute(col_b, "cols", swap_pairs(n_cols, True))

        (toep,) = call(
            band_kernel,
            "band",
            (first_near,),
            (VMEM((DEPTH1, HALF_LANES), bf16),),
            scratch=[pltpu.VMEM((TAPS1, 48, 128), f32)],
            moved=1 << 20,
            limit=4 << 20,
        )
        xb_shape = VMEM((2, BLOCKS, 3, 328, 128), f32)
        fmap_shape = VMEM((BLOCKS, BLOCK_LANES // 128, 104, 128), f32)
        xb, fmap, key_near = call(
            window_kernel,
            "windows",
            (slide_pixels, toep, key_weight),
            (xb_shape, fmap_shape, VMEM(key_weight.shape, bf16)),
            scratch=[pltpu.VMEM((2 * MID_ALL, DEPTH1), bf16), pltpu.SemaphoreType.DMA],
            far=(2,),
            flops=2 * MID_ALL * DEPTH1 * BLOCK_LANES,
            moved=4 << 20,
            limit=8 << 20,
        )
        xb, fmap = call(
            functools.partial(inner_kernel, row_last=n_rows - 1),
            "inner",
            (row_a, row_b, toep, xb, fmap),
            (xb_shape, fmap_shape),
            scratch=[pltpu.VMEM((2 * EDGE_ALL, DEPTH1), bf16)],
            aliases={3: 0, 4: 1},
            flops=2 * EDGE_ALL * DEPTH1 * BLOCK_LANES,
            moved=16 << 20,
            limit=8 << 20,
        )
        smap_shape = VMEM((2, COLS2, ROWS2, 128), f32)
        w2 = stem_second.reshape(2304, 256)
        (smap,) = call(
            middle_kernel,
            "middle",
            (fmap, w2),
            (smap_shape,),
            scratch=[pltpu.VMEM(((COLS2 - 4) * ROWS2, 2304), bf16)],
            flops=2 * COLS2 * ROWS2 * 2304 * 256,
            moved=4 << 20,
            limit=8 << 20,
        )
        _, _, _, normed, value_near = call(
            functools.partial(stem_kernel, col_last=n_cols - 1, row_last=n_rows - 1),
            "stem",
            (
                col_a, col_b, xb, fmap, smap, toep, w2, stem_third.reshape(2304, 1024),
                value_weight,
            ),
            (
                xb_shape, fmap_shape, smap_shape,
                VMEM((128, 1024), bf16), VMEM(value_weight.shape, bf16),
            ),
            scratch=[
                pltpu.VMEM((2 * ROWS1, DEPTH1), bf16),
                pltpu.VMEM((4 * ROWS2, 2304), bf16),
                pltpu.VMEM((128, 2304), bf16),
                pltpu.VMEM((128, 1024), f32),
                pltpu.SemaphoreType.DMA,
            ],
            aliases={2: 0, 3: 1, 4: 2},
            far=(8,),
            flops=2 << 30,
            limit=8 << 20,
        )
        normed_other = lax.ppermute(normed, "rows", swap_pairs(n_rows, False))

        def project(tokens):
            return call(
                project_kernel,
                "project",
                (tokens, key_near, value_near),
                (VMEM((tokens.shape[0], 2048), bf16),),
                flops=1 << 29,
                limit=4 << 20,
            )[0]

        kv, kv_other = project(normed), project(normed_other)
        ordered = order_queries(queries)
        eighth = queries.shape[0] // 8
        width = 1024 + STAT

        def attend(q, keep):
            shape = VMEM((eighth, width), f32 if keep else bf16)
            return call(
                functools.partial(attend_kernel, bit_of=bit_of(0), chunk_of=bit_of(2), keep=keep),
                "attend",
                (q, kv, kv_other),
                (shape, shape),
                flops=1 << 30,
                limit=8 << 20,
            )

        sends = attend(ordered, False)
        ordered, lead, lag = lax.optimization_barrier((ordered, *sends))
        recvs = [exchange(lead, 0), exchange(lag, 0)]
        keeps = list(attend(ordered, True))
        for i in range(2):
            keeps[i], send = merge(keeps[i], recvs[i], bit_of(1))
            recvs[i] = exchange(send, 1)
        recv = exchange(merge(keeps[0], recvs[0], "send"), 2)
        keep = merge(keeps[1], recvs[1], "keep")
        for stage in range(3, len(orders[0])):
            keep, send = merge(keep, recv, bit_of(stage))
            recv = exchange(send, stage)
        return merge(keep, recv, "result")

    placed = (P(None, "rows", "cols"), P(), P(), P(), P(), P(), P())
    return jax.shard_map(
        on_device, mesh=mesh, in_specs=placed, out_specs=P(("cols", "rows"), None), check_vma=False
    )
```

```python
import functools
import math

import jax
import jax.numpy as jnp
from jax import lax
from jax.experimental import pallas as pl
from jax.experimental.pallas import tpu as pltpu
from jax.sharding import PartitionSpec as P

HEADS = 8
BEFORE, AFTER = 21, 5
TAPS1 = 18
BLOCK_COLS = 28
BLOCKS = 5
BLOCK_LANES = BLOCK_COLS * 64
HALF_LANES = BLOCK_LANES // 2
DEPTH1 = TAPS1 * 64
ROWS1 = 80
ROWS2 = 24
COLS2 = 34
STAT = 128
RIM = 24
EDGE, MID = 16, 48
MID_ALL, EDGE_ALL = MID * 5, EDGE * 5 + 48
STRIP = 144
VMEM = pltpu.MemorySpace.VMEM


def gelu(x):
    inner = x * (0.7978845608028654 + 0.035677408136300125 * (x * x))
    half = 0.5 * x
    return half + half * jnp.tanh(inner)


def lanes_of(shape):
    return lax.broadcasted_iota(jnp.int32, shape, len(shape) - 1)


def row_edges_kernel(slide_hbm, kernel_far, a_ref, b_ref, kernel, sems):
    extra = pltpu.make_async_copy(kernel_far, kernel, sems.at[2])
    extra.start()
    even = lax.axis_index("rows") % 2 == 0
    height = slide_hbm.shape[1]

    def send(first, second):
        copies = [
            pltpu.make_async_copy(slide_hbm.at[:, pl.ds(height - RIM, RIM), :], first, sems.at[0]),
            pltpu.make_async_copy(slide_hbm.at[:, pl.ds(0, RIM), :], second, sems.at[1]),
        ]
        for copy in copies:
            copy.start()
        for copy in copies:
            copy.wait()

    @pl.when(even)
    def _():
        send(a_ref, b_ref)

    @pl.when(jnp.logical_not(even))
    def _():
        send(b_ref, a_ref)

    extra.wait()


def rims(c, ra_ref, rb_ref, lanes):
    even = lax.axis_index("rows") % 2 == 0
    ra = ra_ref[c, :, lanes].astype(jnp.float32)
    rb = rb_ref[c, :, lanes].astype(jnp.float32)
    return jnp.where(even, rb, ra), jnp.where(even, ra, rb)[0:8]


def col_edges_kernel(slide, ra_ref, rb_ref, a_ref, b_ref):
    even = lax.axis_index("cols") % 2 == 0
    lane = lanes_of((STRIP, 128))
    first = jnp.zeros((STRIP, 128), jnp.float32)
    last = jnp.zeros((STRIP, 128), jnp.float32)
    for c in range(3):
        sides = []
        for lanes in (slice(0, 128), slice(384, 512)):
            above, below = rims(c, ra_ref, rb_ref, lanes)
            sides.append(jnp.concatenate([above, slide[c, :, lanes].astype(jnp.float32), below], axis=0))
        for half in range(2):
            g = BEFORE * (2 * c + half)
            rows = slice(half * STRIP, half * STRIP + STRIP)
            lo = pltpu.roll(sides[0][rows], g, 1) if g else sides[0][rows]
            hi = pltpu.roll(sides[1][rows], (g + BEFORE) % 128, 1)
            first = jnp.where((lane >= g) & (lane < g + AFTER), lo, first)
            last = jnp.where((lane >= g) & (lane < g + BEFORE), hi, last)
    a_ref[...] = jnp.where(even, last, first).astype(jnp.bfloat16)
    b_ref[...] = jnp.where(even, first, last).astype(jnp.bfloat16)


def band_kernel(kernel_ref, toep, taps):
    taps[...] = jnp.zeros(taps.shape, jnp.float32)
    for kh in range(6):
        for kw in range(6):
            rows = kernel_ref[kh, kw].astype(jnp.float32)
            for c in range(3):
                for top, side in ((0, 0), (4, 1), (24, 0), (28, 1)):
                    taps[6 * c + kh, top + kw : top + kw + 1, 64 * side : 64 * side + 64] = rows[c : c + 1]

    def band(k, carry):
        channel, kh = k // 6, k % 6
        base = pl.multiple_of((3 * channel + kh % 3) * 128 + (kh // 3) * 64, 64)
        toep[pl.ds(base, 64), :] = jnp.zeros((64, HALF_LANES), jnp.bfloat16)
        p0 = taps[k, 0:16, :].astype(jnp.bfloat16)
        p1 = taps[k, 16:32, :].astype(jnp.bfloat16)
        p2 = taps[k, 32:48, :].astype(jnp.bfloat16)
        for m in range(HALF_LANES // 128):
            lanes = slice(128 * m, 128 * m + 128)
            if m % 2 == 0:
                toep[pl.ds(base + 8 * m, 16), lanes] = p0
            else:
                toep[pl.ds(base + 8 * m - 8, 16), lanes] = p1
                toep[pl.ds(base + 8 * m + 8, 16), lanes] = p2
        return carry

    lax.fori_loop(0, TAPS1, band, 0)


def picks(blocks, start):
    lane = lax.broadcasted_iota(jnp.int32, (256, 128), 1)
    source = lax.broadcasted_iota(jnp.int32, (256, 128), 0) + (start + BEFORE)
    out = []
    for b in blocks:
        at = 4 * BLOCK_COLS * b
        for low, high in ((0, 56), (56, 0)):
            want = jnp.where(lane < 64, lane + (at + low), lane + (at + high - 64))
            out.append(jnp.where(source == want, 1.0, 0.0).astype(jnp.bfloat16))
    return jnp.concatenate(out, axis=1)


def cut(rows):
    parts = []
    for blocks, start in (((0, 1), 0), ((2,), 128), ((3, 4), 256)):
        moved = jnp.dot(rows[:, start : start + 256], picks(blocks, start), preferred_element_type=jnp.float32)
        parts += [
            (moved[:, 256 * i : 256 * i + 128], moved[:, 256 * i + 128 : 256 * i + 256]) for i in range(len(blocks))
        ]
    return parts


def patches(xb, b, half, c, pair, start, count):
    low = lanes_of((count, 128)) < 64
    first = xb[half, b, c, pl.ds(RIM - BEFORE + start + pair, count, stride=4), :]
    second = xb[1 - half, b, c, pl.ds(RIM - BEFORE + start + pair + 3, count, stride=4), :]
    return jnp.where(low, first, second)


def window_kernel(slide, toep, w2_far, wk_far, xb, fmap, w2, wk, lhs1, sems):
    copies = [pltpu.make_async_copy(w2_far, w2, sems.at[0]), pltpu.make_async_copy(wk_far, wk, sems.at[1])]
    for copy in copies:
        copy.start()
    for c in range(3):
        for b, part in enumerate(cut(slide[c])):
            for order in range(2):
                xb[order, b, c, RIM : RIM + 256, :] = part[order]
    for half in range(2):
        for b in range(BLOCKS):
            row0 = MID_ALL * half + MID * b
            for k in range(9):
                lhs1[row0 : row0 + MID, 128 * k : 128 * k + 128] = patches(
                    xb, b, half, k // 3, k % 3, 4 * EDGE, MID
                ).astype(jnp.bfloat16)
    for start in range(0, HALF_LANES, 256):
        size = min(256, HALF_LANES - start)
        acc = gelu(jnp.dot(lhs1[...], toep[:, start : start + size], preferred_element_type=jnp.float32))
        for half in range(2):
            for b in range(BLOCKS):
                row0 = MID_ALL * half + MID * b
                for u in range(size // 128):
                    tile = (HALF_LANES * half + start) // 128 + u
                    fmap[b, tile, EDGE : EDGE + MID, :] = acc[row0 : row0 + MID, 128 * u : 128 * u + 128]
    for copy in copies:
        copy.wait()


def inner_kernel(ra_ref, rb_ref, toep, xb_in, fmap_in, xb, fmap, lhs1, *, row_last):
    outer = []
    for c in range(3):
        outer += rims(c, ra_ref, rb_ref, slice(None))
    parts = cut(jnp.concatenate(outer, axis=0).astype(jnp.bfloat16))
    for b in range(BLOCKS):
        for c in range(3):
            for order in range(2):
                xb[order, b, c, 0:RIM, :] = parts[b][order][32 * c : 32 * c + RIM]
                xb[order, b, c, 280:288, :] = parts[b][order][32 * c + RIM : 32 * c + 32]
                xb[order, b, c, 288:328, :] = jnp.zeros((40, 128), jnp.float32)
    for half in range(2):
        top = EDGE_ALL * half
        bottom = top + EDGE * BLOCKS
        for k in range(9):
            lanes = slice(128 * k, 128 * k + 128)
            low = []
            for b in range(BLOCKS):
                lhs1[top + EDGE * b : top + EDGE * b + EDGE, lanes] = patches(
                    xb, b, half, k // 3, k % 3, 0, EDGE
                ).astype(jnp.bfloat16)
                low.append(patches(xb, b, half, k // 3, k % 3, 4 * (EDGE + MID), 8))
            low.append(jnp.zeros((8, 128), jnp.float32))
            lhs1[bottom : bottom + 48, lanes] = jnp.concatenate(low, axis=0).astype(jnp.bfloat16)
    for start in range(0, HALF_LANES, 256):
        size = min(256, HALF_LANES - start)
        acc = gelu(jnp.dot(lhs1[...], toep[:, start : start + size], preferred_element_type=jnp.float32))
        for half in range(2):
            top = EDGE_ALL * half
            bottom = top + EDGE * BLOCKS
            for b in range(BLOCKS):
                for u in range(size // 128):
                    tile = (HALF_LANES * half + start) // 128 + u
                    lanes = slice(128 * u, 128 * u + 128)
                    fmap[b, tile, 0:EDGE, :] = acc[top + EDGE * b : top + EDGE * b + EDGE, lanes]
                    fmap[b, tile, EDGE + MID : EDGE + MID + 8, :] = acc[bottom + 8 * b : bottom + 8 * b + 8, lanes]
    blank_rows(fmap, range(BLOCKS), row_last)


def blank_rows(fmap, blocks, row_last):
    row = lax.axis_index("rows")

    @pl.when(row == 0)
    def _():
        for b in blocks:
            fmap[b, :, 0:5, :] = jnp.zeros((BLOCK_LANES // 128, 5, 128), jnp.float32)

    @pl.when(row == row_last)
    def _():
        for b in blocks:
            fmap[b, :, 69:70, :] = jnp.zeros((BLOCK_LANES // 128, 1, 128), jnp.float32)


def second_map(cols, fmap, w2, lhs2, smap):
    for kh in range(6):
        rows = pl.ds(kh, ROWS2, stride=4)
        for i, col in enumerate(cols):
            for u in range(3):
                tiles = [divmod(2 * j + u, BLOCK_LANES // 128) for j in (col, col + 1)]
                lhs2[48 * i : 48 * i + 48, 384 * kh + 128 * u : 384 * kh + 128 * u + 128] = jnp.concatenate(
                    [fmap[block, tile, rows, :] for block, tile in tiles], axis=0
                ).astype(jnp.bfloat16)
    step = 15
    for start in range(0, len(cols), step):
        some = cols[start : start + step]
        acc = gelu(
            jnp.dot(lhs2[48 * start : 48 * (start + len(some)), :], w2[...], preferred_element_type=jnp.float32)
        )
        for i, col in enumerate(some):
            for u in range(2):
                smap[u, col : col + 2] = acc[48 * i : 48 * i + 48, 128 * u : 128 * u + 128].reshape(2, ROWS2, 128)


def middle_kernel(fmap, w2, smap, lhs2):
    second_map(range(2, COLS2 - 2, 2), fmap, w2, lhs2, smap)


def stem_kernel(
    ca_ref, cb_ref, xb_in, fmap_in, smap_in, toep, w2, w3, far,
    xb, fmap, smap, normed, near,
    lhs1, lhs2, lhs3, third, sem,
    *, col_last, row_last,
):
    copy = pltpu.make_async_copy(far, near, sem)
    copy.start()
    col = lax.axis_index("cols")
    row = lax.axis_index("rows")
    even_col = col % 2 == 0
    lane = lanes_of((STRIP, 128))
    ca = ca_ref[...].astype(jnp.float32)
    cb = cb_ref[...].astype(jnp.float32)
    left_all = jnp.where(even_col, cb, ca)
    right_all = jnp.where(even_col, ca, cb)
    at_right = 512 + BEFORE - 4 * BLOCK_COLS * (BLOCKS - 1) - 56
    for c in range(3):
        for half in range(2):
            g = BEFORE * (2 * c + half)
            rows = slice(half * STRIP, half * STRIP + STRIP)
            for order in range(2):
                at = 64 * order
                left = pltpu.roll(left_all, (at - g) % 128, 1) if at != g else left_all
                here = (lane >= at) & (lane < at + BEFORE)
                xb[order, 0, c, rows, :] = jnp.where(here, left, xb[order, 0, c, rows, :])
                at = at_right + 64 * (1 - order)
                right = pltpu.roll(right_all, (at - g) % 128, 1)
                here = (lane >= at) & (lane < at + AFTER)
                xb[order, BLOCKS - 1, c, rows, :] = jnp.where(here, right, xb[order, BLOCKS - 1, c, rows, :])
    for k in range(9):
        for half, b in ((0, 0), (1, BLOCKS - 1)):
            lhs1[ROWS1 * half : ROWS1 * half + ROWS1, 128 * k : 128 * k + 128] = patches(
                xb, b, half, k // 3, k % 3, 0, ROWS1
            ).astype(jnp.bfloat16)
    for n in range(2):
        acc = gelu(jnp.dot(lhs1[...], toep[:, 256 * n : 256 * n + 256], preferred_element_type=jnp.float32))
        for u in range(2):
            fmap[0, 2 * n + u, 0:ROWS1, :] = acc[0:ROWS1, 128 * u : 128 * u + 128]
    fmap[BLOCKS - 1, 10, 0:ROWS1, :] = acc[ROWS1:, 128:256]

    blank_rows(fmap, (0, BLOCKS - 1), row_last)

    @pl.when(col == 0)
    def _():
        fmap[0, 0:2, 0:ROWS1, :] = jnp.zeros((2, ROWS1, 128), jnp.float32)
        fmap[0, 2, 0:ROWS1, 0:64] = jnp.zeros((ROWS1, 64), jnp.float32)

    @pl.when(col == col_last)
    def _():
        tile, side = divmod(133 - 4 * BLOCK_COLS, 2)
        fmap[4, tile, 0:ROWS1, 64 * side : 64 * side + 64] = jnp.zeros((ROWS1, 64), jnp.float32)

    second_map((0, COLS2 - 2), fmap, w2, lhs2, smap)

    @pl.when(row == 0)
    def _():
        smap[:, :, 0:1, :] = jnp.zeros((2, COLS2, 1, 128), jnp.float32)

    @pl.when(col == 0)
    def _():
        smap[:, 0] = jnp.zeros((2, ROWS2, 128), jnp.float32)

    for kh in range(3):
        for kw in range(3):
            k = 3 * kh + kw
            for pair in range(8):
                for u in range(2):
                    lhs3[16 * pair : 16 * pair + 16, 256 * k + 128 * u : 256 * k + 128 * u + 128] = jnp.concatenate(
                        [
                            smap[u, 4 * pair + 2 * v + kw, pl.ds(kh, 8, stride=2), :]
                            for v in range(2)
                        ],
                        axis=0,
                    ).astype(jnp.bfloat16)

    for n in range(4):
        lanes = slice(256 * n, 256 * n + 256)
        third[:, lanes] = jnp.dot(lhs3[...], w3[:, lanes], preferred_element_type=jnp.float32)
    tokens = third[...]
    centred = tokens - jnp.mean(tokens, axis=-1, keepdims=True)
    var = jnp.mean(centred * centred, axis=-1, keepdims=True)
    normed[...] = (centred * lax.rsqrt(var + 1e-05)).astype(jnp.bfloat16)
    copy.wait()


def project_kernel(tokens, wk, wv, kv):
    for i, w in enumerate((wk, wv)):
        for n in range(4):
            rows = jnp.dot(tokens[...], w[:, 256 * n : 256 * n + 256], preferred_element_type=jnp.float32)
            kv[:, 1024 * i + 256 * n : 1024 * i + 256 * n + 256] = rows.astype(jnp.bfloat16)


def attend_kernel(q, mine, theirs, lead, lag, *, bit_of, chunk_of, keep):
    half = lead.shape[0]
    n = 2 * half
    quarter = 2 * (lax.axis_index("rows") % 2) + (bit_of() if keep else 1 - bit_of())
    rows = pl.ds(pl.multiple_of(quarter * n, n), n)
    upper = chunk_of() == 1

    def put(lanes, value):
        lead[:, lanes] = jnp.where(upper, value[:half], value[half:]).astype(lead.dtype)
        lag[:, lanes] = jnp.where(upper, value[half:], value[:half]).astype(lag.dtype)

    scale = 1.0 / math.sqrt(128)
    lane = lanes_of((n, 128))
    stat = jnp.zeros((n, 128), jnp.float32)
    for h in range(HEADS):
        lanes = slice(128 * h, 128 * h + 128)
        past = slice(1024 + 128 * h, 1024 + 128 * h + 128)
        keys = jnp.concatenate([mine[:, lanes], theirs[:, lanes]], axis=0)
        values = jnp.concatenate([mine[:, past], theirs[:, past]], axis=0)
        scores = lax.dot_general(
            q[rows, lanes], keys, (((1,), (1,)), ((), ())), preferred_element_type=jnp.float32
        ) * scale
        peak = jnp.max(scores, axis=1, keepdims=True)
        w = jnp.exp(scores - peak)
        total = jnp.sum(w, axis=1, keepdims=True)
        o = jnp.dot(w.astype(jnp.bfloat16), values, preferred_element_type=jnp.float32)
        put(lanes, o * (1.0 / total))
        stat = jnp.where(lane == h, peak + jnp.log(total), stat)
    put(slice(1024, 1152), stat if keep else pack_stat(stat).astype(jnp.float32))


def pack_stat(stat):
    lane = lanes_of(stat.shape)
    stat = jnp.where(lane < HEADS, stat, 0.0)
    high = stat.astype(jnp.bfloat16).astype(jnp.float32)
    rest = stat - high
    mid = rest.astype(jnp.bfloat16).astype(jnp.float32)
    low = rest - mid
    return (high + pltpu.roll(mid, HEADS, 1) + pltpu.roll(low, 2 * HEADS, 1)).astype(jnp.bfloat16)


def unpack_stat(stat):
    stat = stat.astype(jnp.float32)
    return stat + pltpu.roll(stat, 128 - HEADS, 1) + pltpu.roll(stat, 128 - 2 * HEADS, 1)


def merge_kernel(keep_ref, recv_ref, *outs, bit_of):
    n = keep_ref.shape[0]
    mine = keep_ref[:, 1024:1152]
    theirs = unpack_stat(recv_ref[:, 1024:1152])
    peak = jnp.maximum(mine, theirs)
    em = jnp.exp(mine - peak)
    total = em + jnp.exp(theirs - peak)
    share = em / total
    stat = peak + jnp.log(total)
    merged = []
    for h in range(HEADS):
        lanes = slice(128 * h, 128 * h + 128)
        a = keep_ref[:, lanes]
        b = recv_ref[:, lanes].astype(jnp.float32)
        merged.append(b + jnp.broadcast_to(share[:, h : h + 1], (n, 128)) * (a - b))
    if not callable(bit_of):
        for h in range(HEADS):
            outs[0][:, 128 * h : 128 * h + 128] = merged[h].astype(outs[0].dtype)
        if bit_of != "result":
            outs[0][:, 1024:1152] = pack_stat(stat) if bit_of == "send" else stat
        return
    upper = bit_of() == 1
    half = n // 2
    for h in range(HEADS):
        lanes = slice(128 * h, 128 * h + 128)
        outs[0][:, lanes] = jnp.where(upper, merged[h][half:], merged[h][:half])
        outs[1][:, lanes] = jnp.where(upper, merged[h][:half], merged[h][half:]).astype(jnp.bfloat16)
    outs[0][:, 1024:1152] = jnp.where(upper, stat[half:], stat[:half])
    outs[1][:, 1024:1152] = pack_stat(jnp.where(upper, stat[:half], stat[half:]))


def call(kernel, name, args, outs, scratch=(), aliases=None, flops=0, moved=0, limit=None, far=()):
    spec = pl.BlockSpec(memory_space=VMEM)
    far_spec = pl.BlockSpec(memory_space=pltpu.HBM)
    return pl.pallas_call(
        kernel,
        in_specs=[far_spec if i in far else spec for i in range(len(args))],
        out_specs=[spec] * len(outs),
        out_shape=tuple(outs),
        scratch_shapes=list(scratch),
        input_output_aliases=aliases or {},
        cost_estimate=pl.CostEstimate(flops=flops, bytes_accessed=moved, transcendentals=0),
        compiler_params=pltpu.CompilerParams(vmem_limit_bytes=limit),
        name=name,
    )(*[pltpu.with_memory_space_constraint(x, pltpu.HBM if i in far else VMEM) for i, x in enumerate(args)])


def merge(keep, recv, bit_of):
    n, width = keep.shape
    if bit_of == "result":
        outs = (jax.ShapeDtypeStruct((n, 1024), jnp.bfloat16),)
    elif not callable(bit_of):
        outs = (VMEM((n, width), jnp.bfloat16 if bit_of == "send" else jnp.float32),)
    else:
        outs = (VMEM((n // 2, width), jnp.float32), VMEM((n // 2, width), jnp.bfloat16))
    out = call(functools.partial(merge_kernel, bit_of=bit_of), "merge", (keep, recv), outs, limit=8 << 20)
    return out if callable(bit_of) else out[0]


def swap_pairs(size, odd):
    pairs = []
    for i in range(1 if odd else 0, size - 1, 2):
        pairs += [(i, i + 1), (i + 1, i)]
    return pairs


def bits_of(size):
    return size.bit_length() - 1


def plan(mesh):
    n_rows, n_cols = mesh.shape["rows"], mesh.shape["cols"]
    row_bits = [("rows", k) for k in range(1, bits_of(n_rows))]
    col_bits = [("cols", k) for k in range(bits_of(n_cols))]
    return row_bits + col_bits, col_bits[:1] + row_bits + col_bits[1:]


def solution(mesh):
    n_rows, n_cols = mesh.shape["rows"], mesh.shape["cols"]
    orders = plan(mesh)

    def partner(index, stage):
        col, row = divmod(index, n_rows)
        axis, k = orders[row & 1][stage]
        return col * n_rows + (row ^ (1 << k)) if axis == "rows" else (col ^ (1 << k)) * n_rows + row

    def exchange(value, stage):
        pairs = [(i, partner(i, stage)) for i in range(n_rows * n_cols)]
        return lax.ppermute(value, ("cols", "rows"), pairs)

    def bit_of(stage):
        def read():
            row = lax.axis_index("rows")
            (axis0, k0), (axis1, k1) = orders[0][stage], orders[1][stage]
            return jnp.where(
                row % 2 == 0, (lax.axis_index(axis0) >> k0) & 1, (lax.axis_index(axis1) >> k1) & 1
            )

        return read

    def order_queries(queries):
        latents, width = queries.shape
        share = latents // (n_rows * n_cols)
        names = [("cols", k) for k in reversed(range(bits_of(n_cols)))]
        names += [("rows", k) for k in reversed(range(bits_of(n_rows)))]
        split = queries.reshape([2] * len(names) + [share, width])
        at = names.index(("rows", 0))
        rest = names[:at] + names[at + 1 :]
        halves = []
        for core in range(2):
            part = lax.index_in_dim(split, core, at, keepdims=False)
            order = orders[core]
            axes = [rest.index(name) for name in order[:1] + order[2:3] + order[1:2] + order[3:]]
            halves.append(part.transpose(axes + [len(rest), len(rest) + 1]).reshape(latents // 2, width))
        return jnp.concatenate(halves, axis=0)

    def on_device(slide_pixels, stem_first, stem_second, stem_third, key_weight, value_weight, queries):
        bf16, f32 = jnp.bfloat16, jnp.float32
        rim = VMEM((3, RIM, 512), bf16)
        row_a, row_b, first_near = call(
            row_edges_kernel,
            "row_edges",
            (slide_pixels, stem_first),
            (rim, rim, VMEM(stem_first.shape, bf16)),
            scratch=[pltpu.SemaphoreType.DMA((3,))],
            limit=8 << 20,
            far=(0, 1),
        )
        row_a = lax.ppermute(row_a, "rows", swap_pairs(n_rows, False))
        row_b = lax.ppermute(row_b, "rows", swap_pairs(n_rows, True))
        strip = VMEM((STRIP, 128), bf16)
        col_a, col_b = call(
            col_edges_kernel, "col_edges", (slide_pixels, row_a, row_b), (strip, strip), limit=8 << 20
        )
        col_a = lax.ppermute(col_a, "cols", swap_pairs(n_cols, False))
        col_b = lax.ppermute(col_b, "cols", swap_pairs(n_cols, True))

        (toep,) = call(
            band_kernel,
            "band",
            (first_near,),
            (VMEM((DEPTH1, HALF_LANES), bf16),),
            scratch=[pltpu.VMEM((TAPS1, 48, 128), f32)],
            moved=1 << 20,
            limit=4 << 20,
        )
        xb_shape = VMEM((2, BLOCKS, 3, 328, 128), f32)
        fmap_shape = VMEM((BLOCKS, BLOCK_LANES // 128, 104, 128), f32)
        xb, fmap, w2, key_near = call(
            window_kernel,
            "windows",
            (slide_pixels, toep, stem_second.reshape(2304, 256), key_weight),
            (xb_shape, fmap_shape, VMEM((2304, 256), bf16), VMEM(key_weight.shape, bf16)),
            scratch=[pltpu.VMEM((2 * MID_ALL, DEPTH1), bf16), pltpu.SemaphoreType.DMA((2,))],
            far=(2, 3),
            flops=2 * MID_ALL * DEPTH1 * BLOCK_LANES,
            moved=4 << 20,
            limit=8 << 20,
        )
        xb, fmap = call(
            functools.partial(inner_kernel, row_last=n_rows - 1),
            "inner",
            (row_a, row_b, toep, xb, fmap),
            (xb_shape, fmap_shape),
            scratch=[pltpu.VMEM((2 * EDGE_ALL, DEPTH1), bf16)],
            aliases={3: 0, 4: 1},
            flops=2 * EDGE_ALL * DEPTH1 * BLOCK_LANES,
            moved=16 << 20,
            limit=8 << 20,
        )
        smap_shape = VMEM((2, COLS2, ROWS2, 128), f32)
        (smap,) = call(
            middle_kernel,
            "middle",
            (fmap, w2),
            (smap_shape,),
            scratch=[pltpu.VMEM(((COLS2 - 4) * ROWS2, 2304), bf16)],
            flops=2 * COLS2 * ROWS2 * 2304 * 256,
            moved=4 << 20,
            limit=8 << 20,
        )
        _, _, _, normed, value_near = call(
            functools.partial(stem_kernel, col_last=n_cols - 1, row_last=n_rows - 1),
            "stem",
            (
                col_a, col_b, xb, fmap, smap, toep, w2, stem_third.reshape(2304, 1024),
                value_weight,
            ),
            (
                xb_shape, fmap_shape, smap_shape,
                VMEM((128, 1024), bf16), VMEM(value_weight.shape, bf16),
            ),
            scratch=[
                pltpu.VMEM((2 * ROWS1, DEPTH1), bf16),
                pltpu.VMEM((4 * ROWS2, 2304), bf16),
                pltpu.VMEM((128, 2304), bf16),
                pltpu.VMEM((128, 1024), f32),
                pltpu.SemaphoreType.DMA,
            ],
            aliases={2: 0, 3: 1, 4: 2},
            far=(8,),
            flops=2 << 30,
            limit=8 << 20,
        )
        normed_other = lax.ppermute(normed, "rows", swap_pairs(n_rows, False))

        def project(tokens):
            return call(
                project_kernel,
                "project",
                (tokens, key_near, value_near),
                (VMEM((tokens.shape[0], 2048), bf16),),
                flops=1 << 29,
                limit=4 << 20,
            )[0]

        kv, kv_other = project(normed), project(normed_other)
        ordered = order_queries(queries)
        eighth = queries.shape[0] // 8
        width = 1024 + STAT

        def attend(q, keep):
            shape = VMEM((eighth, width), f32 if keep else bf16)
            return call(
                functools.partial(attend_kernel, bit_of=bit_of(0), chunk_of=bit_of(2), keep=keep),
                "attend",
                (q, kv, kv_other),
                (shape, shape),
                flops=1 << 30,
                limit=8 << 20,
            )

        sends = attend(ordered, False)
        ordered, lead, lag = lax.optimization_barrier((ordered, *sends))
        recvs = [exchange(lead, 0), exchange(lag, 0)]
        keeps = list(attend(ordered, True))
        for i in range(2):
            keeps[i], send = merge(keeps[i], recvs[i], bit_of(1))
            recvs[i] = exchange(send, 1)
        recv = exchange(merge(keeps[0], recvs[0], "send"), 2)
        keep = merge(keeps[1], recvs[1], "keep")
        for stage in range(3, len(orders[0])):
            keep, send = merge(keep, recv, bit_of(stage))
            recv = exchange(send, stage)
        return merge(keep, recv, "result")

    placed = (P(None, "rows", "cols"), P(), P(), P(), P(), P(), P())
    return jax.shard_map(
        on_device, mesh=mesh, in_specs=placed, out_specs=P(("cols", "rows"), None), check_vma=False
    )
```
